256 devices in a mesh: dp: 4 (over x), tm: 32 (over z, y), height: 2 (over core).
Axes of the slice: x: 4, y: 4, z: 8, core: 2. Of those that a mesh axis runs over, the one named last changes fastest.
Arguments:
- clip_frames: bfloat16 [128, 64, 160, 256], P(('dp', 'tm'), 'height'), parts along dimension 0
- frame_of_slot: int32 [128], P('dp'), parts along dimension 0, may hold values from -1 to 16, as said below
- w_spatial: bfloat16 [3, 3, 256, 512], replicated, may hold values from -0.125 to 0.125
- norm_gain: float32 [512], replicated, may hold values from 0.1 to 1.9
- norm_shift: float32 [512], replicated, may hold values from -3 to 3
- w_time: bfloat16 [3, 512, 512], replicated, may hold values from -0.15625 to 0.15625
- time_bias: float32 [512], replicated, may hold values from -3 to 3
Outputs:
- latent: bfloat16 [36, 2, 32, 160, 512], P('dp', 'height', 'tm'), parts along dimension 0
The draws below stay inside these ranges and needn't reach their ends.
There are 4 independent parts, one for each index of `dp`. The reference program is written for one: setup_inputs(seed, part) draws one part's arguments, and reference() takes and returns one part's arrays. A program takes and returns all parts, laid end to end along the dimension named above; an argument that names none is the same for every part. Nothing has to cross between parts.
Inputs may be any that keep to these rules, and one draw needn't show every extreme that they name: `frame_of_slot`: each frame 0 to 16 stands in exactly one slot; every other slot holds -1.
All inputs are finite; a program needn't handle non-finite values.
Results may differ from the reference program's by a relative error of at most 0.0053.
Values may be sent and summed in bfloat16 or wider, within the bound.
A program may use at most 192 MiB of HBM per device.

```python
import jax
import jax.numpy as jnp
from jax import lax

CIN = 256
COUT = 512
GROUPS = 32
RH = 32
W = 160
H = 64
LIVE = 17
OUTF = 9
N_TM = 32
N_HEIGHT = 2


def draw_frame_of_slot(key, part):
    shuffled = jax.random.permutation(jax.random.fold_in(key, 7), N_TM)
    inverse = jnp.zeros((N_TM,), jnp.int32).at[shuffled].set(jnp.arange(N_TM, dtype=jnp.int32))
    return jnp.where(inverse < LIVE, inverse, -1).astype(jnp.int32)


def draw_clip_frames(key, part):
    key_base = jax.random.fold_in(key, 11)
    key_slot = jax.random.fold_in(key, 12)
    key_row = jax.random.fold_in(key, 13)
    key_chan = jax.random.fold_in(key, 14)
    slot_scale = jnp.exp(jax.random.uniform(key_slot, (N_TM, 1, 1, 1), jnp.float32, -0.69, 0.69))
    row_pos = jnp.arange(H, dtype=jnp.float32).reshape(1, H, 1, 1) / (H - 1)
    row_scale = (1.0 + 2.0 * row_pos) * jnp.exp(jax.random.uniform(key_row, (1, H, 1, 1), jnp.float32, -0.35, 0.35))
    chan_scale = jnp.exp(jax.random.uniform(key_chan, (1, 1, 1, CIN), jnp.float32, -1.2, 1.15))
    base = jnp.clip(jax.random.normal(key_base, (N_TM, H, W, CIN), jnp.float32), -5.0, 5.0)
    return (base * slot_scale * row_scale * chan_scale).astype(jnp.bfloat16)


def noise(key, dims, width, most, held_as=jnp.bfloat16):
    result = width * jax.random.normal(key, dims, jnp.float32)
    return jnp.clip(result, min=-most, max=most).astype(held_as)


def setup_inputs(seed: int = 0, part: int = 0) -> dict:
    seeds = jax.random.split(jax.random.key(seed), 8)
    own_keys = jax.random.split(jax.random.fold_in(seeds[7], part), 8)
    clip_frames = draw_clip_frames(jax.random.fold_in(jax.random.fold_in(seeds[7], part), 71), part)
    frame_of_slot = draw_frame_of_slot(jax.random.fold_in(jax.random.fold_in(seeds[7], part), 71), part)
    w_spatial = noise(seeds[2], (3, 3, CIN, COUT), (9 * CIN) ** -0.5, 0.125)
    norm_gain = jnp.clip(1.0 + 0.18 * jax.random.normal(seeds[3], (COUT,), jnp.float32), 0.1, 1.9)
    norm_shift = noise(seeds[4], (COUT,), 0.5, 3.0, jnp.float32)
    w_time = noise(seeds[5], (3, COUT, COUT), (3 * COUT) ** -0.5, 0.15625)
    time_bias = noise(seeds[6], (COUT,), 0.5, 3.0, jnp.float32)
    return {"clip_frames": clip_frames, "frame_of_slot": frame_of_slot, "w_spatial": w_spatial, "norm_gain": norm_gain, "norm_shift": norm_shift, "w_time": w_time, "time_bias": time_bias}


def conv_frame(one_frame, w_spatial):
    padded = jnp.pad(one_frame, ((1, 1), (1, 1), (0, 0)))
    running = jnp.zeros((H * W, COUT), jnp.float32)
    for row_tap in range(3):
        for col_tap in range(3):
            window = padded[row_tap:row_tap + H, col_tap:col_tap + W].reshape(H * W, CIN)
            running = running + jnp.dot(window, w_spatial[row_tap, col_tap], preferred_element_type=jnp.float32)
    return running.reshape(H, W, COUT).astype(jnp.bfloat16)

def reference(clip_frames, frame_of_slot, w_spatial, norm_gain, norm_shift, w_time, time_bias):
    wanted = jnp.arange(LIVE, dtype=jnp.int32)[:, None]
    places = jnp.arange(N_TM, dtype=jnp.int32)[None, :]
    matches = frame_of_slot[None, :] == wanted
    frame_slots = lax.optimization_barrier(jnp.sum(jnp.where(matches, places, 0), axis=1)).astype(jnp.int32)
    frames = jnp.take(clip_frames, frame_slots, axis=0)
    conv_out = lax.map(lambda one_frame: conv_frame(one_frame, w_spatial), frames)
    per_group = COUT // GROUPS
    values = conv_out.astype(jnp.float32)
    grouped = values.reshape(LIVE, H, W, GROUPS, per_group)
    group_mean = lax.optimization_barrier(jnp.mean(grouped, axis=(0, 1, 2, 4)))
    group_sq = lax.optimization_barrier(jnp.mean(grouped * grouped, axis=(0, 1, 2, 4)))
    group_var = group_sq - group_mean * group_mean
    inv_scale = lax.rsqrt(group_var + 1e-06)
    mean_chan = jnp.repeat(group_mean, per_group)
    scale_chan = jnp.repeat(inv_scale, per_group)
    activated = jax.nn.silu((values - mean_chan) * scale_chan * norm_gain + norm_shift).astype(jnp.bfloat16)
    outputs = []
    for out_step in range(OUTF):
        running = jnp.zeros((H * W, COUT), jnp.float32) + time_bias
        for time_tap in range(3):
            source = max(2 * out_step + time_tap - 2, 0)
            running = running + jnp.dot(activated[source].reshape(H * W, COUT), w_time[time_tap], preferred_element_type=jnp.float32)
        outputs.append(running.astype(jnp.bfloat16))
    latent = jnp.stack(outputs, axis=0)
    return latent.reshape(OUTF, N_HEIGHT, RH, W, COUT)
```

```python
import jax
import jax.numpy as jnp
import numpy as np
from jax import lax
from jax.sharding import PartitionSpec as P

GROUPS = 32


def with_halo(block, sides, width):
    for axis, dim in sides:
        count = lax.axis_size(axis)
        forward = [(i, i + 1) for i in range(count - 1)]
        backward = [(target, source) for source, target in forward]
        low = lax.ppermute(
            lax.slice_in_dim(block, block.shape[dim] - width, None, axis=dim), axis, forward
        )
        high = lax.ppermute(lax.slice_in_dim(block, 0, width, axis=dim), axis, backward)
        block = jnp.concatenate([low, block, high], axis=dim)
    return block


def slot_lookup(frame_of_slot, live_frames):
    wanted = jnp.arange(live_frames, dtype=jnp.int32)[:, None]
    places = jnp.arange(frame_of_slot.shape[0], dtype=jnp.int32)[None, :]
    matches = frame_of_slot[None, :] == wanted
    return jnp.sum(jnp.where(matches, places, 0), axis=1)


def spatial_conv(row_padded, w_spatial):
    out = lax.conv_general_dilated(
        row_padded,
        w_spatial,
        window_strides=(1, 1),
        padding=((0, 0), (1, 1)),
        dimension_numbers=("NHWC", "HWIO", "NHWC"),
        preferred_element_type=jnp.float32,
    )
    return out.astype(jnp.bfloat16)


def group_stats(conv_out, weight):
    cout_width = conv_out.shape[-1]
    per_group = cout_width // GROUPS
    values = conv_out.astype(jnp.float32).reshape(-1, cout_width)
    sums = jnp.sum(values, axis=0).reshape(GROUPS, per_group).sum(axis=1) * weight
    squares = jnp.sum(values * values, axis=0).reshape(GROUPS, per_group).sum(axis=1) * weight
    return sums, squares


def normalize(conv_out, sums, squares, cell_count, norm_gain, norm_shift):
    per_group = conv_out.shape[-1] // GROUPS
    group_mean = sums / cell_count
    group_var = squares / cell_count - group_mean * group_mean
    inv_scale = lax.rsqrt(group_var + 1e-06)
    mean_chan = jnp.repeat(group_mean, per_group)
    scale_chan = jnp.repeat(inv_scale, per_group)
    values = conv_out.astype(jnp.float32)
    return jax.nn.silu((values - mean_chan) * scale_chan * norm_gain + norm_shift).astype(
        jnp.bfloat16
    )


def time_conv(activated, w_time, time_bias, out_frames):
    running = None
    for time_tap in range(3):
        sources = np.array(
            [max(2 * out_step + time_tap - 2, 0) for out_step in range(out_frames)], np.int32
        )
        picked = jnp.take(activated, jnp.asarray(sources), axis=0)
        product = jnp.einsum(
            "trwc,cd->trwd", picked, w_time[time_tap], preferred_element_type=jnp.float32
        )
        running = product if running is None else running + product
    return (running + time_bias).astype(jnp.bfloat16)


def shards(clip_frames, frame_of_slot, w_spatial, norm_gain, norm_shift, w_time, time_bias):
    tm_count = lax.axis_size("tm")
    height_count = lax.axis_size("height")
    live_frames = tm_count // 2 + 1
    out_frames = (live_frames - 1) // 2 + 1
    frame_slots = slot_lookup(frame_of_slot, live_frames)
    padded = with_halo(clip_frames, (("height", 1),), 1)
    conv_out = spatial_conv(padded, w_spatial)
    exchanged = lax.all_to_all(conv_out, "tm", split_axis=1, concat_axis=0, tiled=True)
    own_frame = lax.dynamic_index_in_dim(frame_of_slot, lax.axis_index("tm"), 0, keepdims=False)
    weight = jnp.where(own_frame >= 0, 1.0, 0.0).astype(jnp.float32)
    sums, squares = group_stats(conv_out, weight)
    sums, squares = lax.psum((sums, squares), ("tm", "height"))
    per_group = conv_out.shape[-1] // GROUPS
    cell_count = float(
        live_frames * clip_frames.shape[1] * height_count * conv_out.shape[2] * per_group
    )
    live = jnp.take(exchanged, frame_slots, axis=0)
    activated = normalize(live, sums, squares, cell_count, norm_gain, norm_shift)
    latent = time_conv(activated, w_time, time_bias, out_frames)
    return latent.reshape(out_frames, 1, latent.shape[1], latent.shape[2], latent.shape[3])


def solution(mesh):
    return jax.shard_map(
        shards,
        mesh=mesh,
        in_specs=(P(("dp", "tm"), "height", None, None), P("dp"), P(), P(), P(), P(), P()),
        out_specs=P("dp", "height", "tm", None, None),
        check_vma=False,
    )
```

```python
import jax
import jax.numpy as jnp
import numpy as np
from jax import lax
from jax.sharding import PartitionSpec as P

GROUPS = 32


def with_halo(block, sides, width):
    for axis, dim in sides:
        count = lax.axis_size(axis)
        forward = [(i, i + 1) for i in range(count - 1)]
        backward = [(target, source) for source, target in forward]
        low = lax.ppermute(
            lax.slice_in_dim(block, block.shape[dim] - width, None, axis=dim), axis, forward
        )
        high = lax.ppermute(lax.slice_in_dim(block, 0, width, axis=dim), axis, backward)
        block = jnp.concatenate([low, block, high], axis=dim)
    return block


def slot_lookup(frame_of_slot, live_frames):
    wanted = jnp.arange(live_frames, dtype=jnp.int32)[:, None]
    places = jnp.arange(frame_of_slot.shape[0], dtype=jnp.int32)[None, :]
    matches = frame_of_slot[None, :] == wanted
    return jnp.sum(jnp.where(matches, places, 0), axis=1)


def spatial_conv(row_padded, w_spatial):
    out = lax.conv_general_dilated(
        row_padded,
        w_spatial,
        window_strides=(1, 1),
        padding=((0, 0), (1, 1)),
        dimension_numbers=("NHWC", "HWIO", "NHWC"),
        preferred_element_type=jnp.float32,
    )
    return out.astype(jnp.bfloat16)


def group_stats(conv_out, weight):
    cout_width = conv_out.shape[-1]
    per_group = cout_width // GROUPS
    values = conv_out.astype(jnp.float32).reshape(-1, cout_width)
    sums = jnp.sum(values, axis=0).reshape(GROUPS, per_group).sum(axis=1) * weight
    squares = jnp.sum(values * values, axis=0).reshape(GROUPS, per_group).sum(axis=1) * weight
    return sums, squares


def normalize(conv_out, sums, squares, cell_count, norm_gain, norm_shift):
    per_group = conv_out.shape[-1] // GROUPS
    group_mean = sums / cell_count
    group_var = squares / cell_count - group_mean * group_mean
    inv_scale = lax.rsqrt(group_var + 1e-06)
    mean_chan = jnp.repeat(group_mean, per_group)
    scale_chan = jnp.repeat(inv_scale, per_group)
    values = conv_out.astype(jnp.float32)
    return jax.nn.silu((values - mean_chan) * scale_chan * norm_gain + norm_shift).astype(
        jnp.bfloat16
    )


def time_conv(activated, w_time, time_bias, out_frames):
    first = activated[0:1]
    even = activated[0::2][:out_frames]
    odd = activated[1::2][: out_frames - 1]
    taps = [
        jnp.concatenate([first, even[: out_frames - 1]], axis=0),
        jnp.concatenate([first, odd], axis=0),
        even,
    ]
    stacked = jnp.concatenate(taps, axis=-1)
    weights = w_time.reshape(-1, w_time.shape[-1])
    product = jnp.einsum("trwc,cd->trwd", stacked, weights, preferred_element_type=jnp.float32)
    return (product + time_bias).astype(jnp.bfloat16)


def encode_stats(stats):
    high = stats.astype(jnp.bfloat16)
    low = (stats - high.astype(jnp.float32)).astype(jnp.bfloat16)
    return jnp.concatenate([high, low])


def decode_stats(coded, width):
    values = coded.astype(jnp.float32)
    return jnp.sum(values[:, :width], axis=0) + jnp.sum(values[:, width : 2 * width], axis=0)


def shards(clip_frames, frame_of_slot, w_spatial, norm_gain, norm_shift, w_time, time_bias):
    tm_count = lax.axis_size("tm")
    height_count = lax.axis_size("height")
    live_frames = tm_count // 2 + 1
    out_frames = (live_frames - 1) // 2 + 1
    frame_slots = slot_lookup(frame_of_slot, live_frames)
    padded = with_halo(clip_frames, (("height", 1),), 1)
    conv_out = spatial_conv(padded, w_spatial)
    own_frame = lax.dynamic_index_in_dim(frame_of_slot, lax.axis_index("tm"), 0, keepdims=False)
    weight = jnp.where(own_frame >= 0, 1.0, 0.0).astype(jnp.float32)
    sums, squares = group_stats(conv_out, weight)
    coded = encode_stats(jnp.concatenate([sums, squares]))
    column = jnp.zeros((conv_out.shape[-1],), jnp.bfloat16).at[: coded.shape[0]].set(coded)
    column = jnp.broadcast_to(column, (1, conv_out.shape[1], 1, conv_out.shape[-1]))
    payload = jnp.concatenate([conv_out, column], axis=2)
    received = lax.all_to_all(payload, "tm", split_axis=1, concat_axis=0, tiled=True)
    exchanged = received[:, :, : conv_out.shape[2]]
    partial = decode_stats(received[:, 0, conv_out.shape[2], : coded.shape[0]], 2 * GROUPS)
    other = lax.ppermute(partial, "height", [(0, 1), (1, 0)])
    totals = partial + other
    sums, squares = totals[:GROUPS], totals[GROUPS:]
    per_group = conv_out.shape[-1] // GROUPS
    cell_count = float(
        live_frames * clip_frames.shape[1] * height_count * conv_out.shape[2] * per_group
    )
    live = jnp.take(exchanged, frame_slots, axis=0)
    activated = normalize(live, sums, squares, cell_count, norm_gain, norm_shift)
    latent = time_conv(activated, w_time, time_bias, out_frames)
    return latent.reshape(out_frames, 1, latent.shape[1], latent.shape[2], latent.shape[3])


def solution(mesh):
    return jax.shard_map(
        shards,
        mesh=mesh,
        in_specs=(P(("dp", "tm"), "height", None, None), P("dp"), P(), P(), P(), P(), P()),
        out_specs=P("dp", "height", "tm", None, None),
        check_vma=False,
    )
```

```python
import jax
import jax.numpy as jnp
import numpy as np
from jax import lax
from jax.sharding import PartitionSpec as P

GROUPS = 32


def with_halo(block, sides, width):
    for axis, dim in sides:
        count = lax.axis_size(axis)
        forward = [(i, i + 1) for i in range(count - 1)]
        backward = [(target, source) for source, target in forward]
        low = lax.ppermute(
            lax.slice_in_dim(block, block.shape[dim] - width, None, axis=dim), axis, forward
        )
        high = lax.ppermute(lax.slice_in_dim(block, 0, width, axis=dim), axis, backward)
        block = jnp.concatenate([low, block, high], axis=dim)
    return block


def slot_lookup(frame_of_slot, live_frames):
    wanted = jnp.arange(live_frames, dtype=jnp.int32)[:, None]
    places = jnp.arange(frame_of_slot.shape[0], dtype=jnp.int32)[None, :]
    matches = frame_of_slot[None, :] == wanted
    return jnp.sum(jnp.where(matches, places, 0), axis=1)


def spatial_conv(row_padded, w_spatial):
    out = lax.conv_general_dilated(
        row_padded,
        w_spatial,
        window_strides=(1, 1),
        padding=((0, 0), (1, 1)),
        dimension_numbers=("NHWC", "HWIO", "NHWC"),
        preferred_element_type=jnp.float32,
    )
    return out.astype(jnp.bfloat16)


def group_stats(conv_out, weight):
    cout_width = conv_out.shape[-1]
    per_group = cout_width // GROUPS
    values = conv_out.astype(jnp.float32).reshape(-1, cout_width)
    sums = jnp.sum(values, axis=0).reshape(GROUPS, per_group).sum(axis=1) * weight
    squares = jnp.sum(values * values, axis=0).reshape(GROUPS, per_group).sum(axis=1) * weight
    return sums, squares


def normalize(conv_out, sums, squares, cell_count, norm_gain, norm_shift):
    per_group = conv_out.shape[-1] // GROUPS
    group_mean = sums / cell_count
    group_var = squares / cell_count - group_mean * group_mean
    inv_scale = lax.rsqrt(group_var + 1e-06)
    mean_chan = jnp.repeat(group_mean, per_group)
    scale_chan = jnp.repeat(inv_scale, per_group)
    values = conv_out.astype(jnp.float32)
    return jax.nn.silu((values - mean_chan) * scale_chan * norm_gain + norm_shift).astype(
        jnp.bfloat16
    )


def time_conv(activated, w_time, time_bias, out_frames):
    first = activated[0:1]
    even = activated[0::2][:out_frames]
    odd = activated[1::2][: out_frames - 1]
    taps = [
        jnp.concatenate([first, even[: out_frames - 1]], axis=0),
        jnp.concatenate([first, odd], axis=0),
        even,
    ]
    stacked = jnp.concatenate(taps, axis=-1)
    weights = w_time.reshape(-1, w_time.shape[-1])
    product = jnp.einsum("trwc,cd->trwd", stacked, weights, preferred_element_type=jnp.float32)
    return (product + time_bias).astype(jnp.bfloat16)


def encode_stats(stats):
    high = stats.astype(jnp.bfloat16)
    low = (stats - high.astype(jnp.float32)).astype(jnp.bfloat16)
    return jnp.concatenate([high, low])


def decode_stats(coded, width):
    values = coded.astype(jnp.float32)
    return jnp.sum(values[:, :width], axis=0) + jnp.sum(values[:, width : 2 * width], axis=0)


def shards(clip_frames, frame_of_slot, w_spatial, norm_gain, norm_shift, w_time, time_bias):
    tm_count = lax.axis_size("tm")
    height_count = lax.axis_size("height")
    live_frames = tm_count // 2 + 1
    out_frames = (live_frames - 1) // 2 + 1
    frame_slots = slot_lookup(frame_of_slot, live_frames)
    padded = with_halo(clip_frames, (("height", 1),), 1)
    conv_out = spatial_conv(padded, w_spatial)
    own_frame = lax.dynamic_index_in_dim(frame_of_slot, lax.axis_index("tm"), 0, keepdims=False)
    weight = jnp.where(own_frame >= 0, 1.0, 0.0).astype(jnp.float32)
    sums, squares = group_stats(conv_out, weight)
    coded = encode_stats(jnp.concatenate([sums, squares]))
    lanes = 128
    rows, cols, chans = conv_out.shape[1], conv_out.shape[2], conv_out.shape[3]
    column = jnp.zeros((lanes,), jnp.bfloat16).at[: coded.shape[0]].set(coded)
    column = jnp.broadcast_to(column, (1, rows, 1, lanes))
    flat = conv_out.reshape(1, rows, cols * chans // lanes, lanes)
    payload = jnp.concatenate([flat, column], axis=2)
    received = lax.all_to_all(payload, "tm", split_axis=1, concat_axis=0, tiled=True)
    exchanged = received[:, :, : cols * chans // lanes].reshape(received.shape[0], 1, cols, chans)
    partial = decode_stats(received[:, 0, cols * chans // lanes, : coded.shape[0]], 2 * GROUPS)
    other = lax.ppermute(partial, "height", [(0, 1), (1, 0)])
    totals = partial + other
    sums, squares = totals[:GROUPS], totals[GROUPS:]
    per_group = conv_out.shape[-1] // GROUPS
    cell_count = float(
        live_frames * clip_frames.shape[1] * height_count * conv_out.shape[2] * per_group
    )
    live = jnp.take(exchanged, frame_slots, axis=0)
    activated = normalize(live, sums, squares, cell_count, norm_gain, norm_shift)
    latent = time_conv(activated, w_time, time_bias, out_frames)
    return latent.reshape(out_frames, 1, latent.shape[1], latent.shape[2], latent.shape[3])


def solution(mesh):
    return jax.shard_map(
        shards,
        mesh=mesh,
        in_specs=(P(("dp", "tm"), "height", None, None), P("dp"), P(), P(), P(), P(), P()),
        out_specs=P("dp", "height", "tm", None, None),
        check_vma=False,
    )
```

```python
import functools

import jax
import jax.numpy as jnp
import numpy as np
from jax import lax
from jax.experimental import pallas as pl
from jax.experimental.pallas import tpu as pltpu
from jax.sharding import PartitionSpec as P

GROUPS = 32


def with_halo(block, sides, width):
    for axis, dim in sides:
        count = lax.axis_size(axis)
        forward = [(i, i + 1) for i in range(count - 1)]
        backward = [(target, source) for source, target in forward]
        low = lax.ppermute(
            lax.slice_in_dim(block, block.shape[dim] - width, None, axis=dim), axis, forward
        )
        high = lax.ppermute(lax.slice_in_dim(block, 0, width, axis=dim), axis, backward)
        block = jnp.concatenate([low, block, high], axis=dim)
    return block


def slot_lookup(frame_of_slot, live_frames):
    wanted = jnp.arange(live_frames, dtype=jnp.int32)[:, None]
    places = jnp.arange(frame_of_slot.shape[0], dtype=jnp.int32)[None, :]
    matches = frame_of_slot[None, :] == wanted
    return jnp.sum(jnp.where(matches, places, 0), axis=1)


def conv_kernel(x_ref, w_ref, out_ref, sum_ref, sq_ref, *, chunk, cols):
    step = pl.program_id(0)
    base = step * chunk
    m = chunk * cols
    parts = []
    for col_tap in range(3):
        acc = None
        for row_tap in range(3):
            xs = x_ref[pl.ds(base + row_tap, chunk), :, :].reshape(m, x_ref.shape[-1])
            p = jnp.dot(xs, w_ref[row_tap, col_tap], preferred_element_type=jnp.float32)
            acc = p if acc is None else acc + p
        parts.append(acc)
    col = lax.broadcasted_iota(jnp.int32, (m, 1), 0) % cols
    left = jnp.where(col == 0, 0.0, pltpu.roll(parts[0], 1, 0))
    right = jnp.where(col == cols - 1, 0.0, pltpu.roll(parts[2], m - 1, 0))
    total = (left + parts[1]) + right
    rounded = total.astype(jnp.bfloat16)
    out_ref[:, 0:cols, :] = rounded.reshape(chunk, cols, -1)
    out_ref[:, cols:cols + 1, :] = jnp.zeros((chunk, 1, out_ref.shape[-1]), jnp.bfloat16)
    values = rounded.astype(jnp.float32)

    @pl.when(step == 0)
    def _():
        sum_ref[...] = jnp.zeros_like(sum_ref)
        sq_ref[...] = jnp.zeros_like(sq_ref)

    sum_ref[...] += jnp.sum(values, axis=0, keepdims=True)
    sq_ref[...] += jnp.sum(values * values, axis=0, keepdims=True)

def conv_call(x, w, chunk=8):
    rows = x.shape[0] - 2
    cols = x.shape[1]
    cin = x.shape[2]
    cout = w.shape[-1]
    return pl.pallas_call(
        functools.partial(conv_kernel, chunk=chunk, cols=cols),
        grid=(rows // chunk,),
        in_specs=[
            pl.BlockSpec((rows + 2, cols, cin), lambda i: (0, 0, 0)),
            pl.BlockSpec((3, 3, cin, cout), lambda i: (0, 0, 0, 0)),
        ],
        out_specs=[
            pl.BlockSpec((chunk, cols + 1, cout), lambda i: (i, 0, 0)),
            pl.BlockSpec((1, cout), lambda i: (0, 0)),
            pl.BlockSpec((1, cout), lambda i: (0, 0)),
        ],
        out_shape=[
            jax.ShapeDtypeStruct((rows, cols + 1, cout), jnp.bfloat16),
            jax.ShapeDtypeStruct((1, cout), jnp.float32),
            jax.ShapeDtypeStruct((1, cout), jnp.float32),
        ],
        compiler_params=pltpu.CompilerParams(dimension_semantics=("arbitrary",)),
    )(x, w)


def spatial_conv(row_padded, w_spatial):
    out = lax.conv_general_dilated(
        row_padded,
        w_spatial,
        window_strides=(1, 1),
        padding=((0, 0), (1, 1)),
        dimension_numbers=("NHWC", "HWIO", "NHWC"),
        preferred_element_type=jnp.float32,
    )
    return out.astype(jnp.bfloat16)


def group_stats(conv_out, weight):
    cout_width = conv_out.shape[-1]
    per_group = cout_width // GROUPS
    values = conv_out.astype(jnp.float32).reshape(-1, cout_width)
    sums = jnp.sum(values, axis=0).reshape(GROUPS, per_group).sum(axis=1) * weight
    squares = jnp.sum(values * values, axis=0).reshape(GROUPS, per_group).sum(axis=1) * weight
    return sums, squares


def normalize(conv_out, sums, squares, cell_count, norm_gain, norm_shift):
    per_group = conv_out.shape[-1] // GROUPS
    group_mean = sums / cell_count
    group_var = squares / cell_count - group_mean * group_mean
    inv_scale = lax.rsqrt(group_var + 1e-06)
    mean_chan = jnp.repeat(group_mean, per_group)
    scale_chan = jnp.repeat(inv_scale, per_group)
    values = conv_out.astype(jnp.float32)
    return jax.nn.silu((values - mean_chan) * scale_chan * norm_gain + norm_shift).astype(
        jnp.bfloat16
    )


def time_conv(activated, w_time, time_bias, out_frames):
    first = activated[0:1]
    even = activated[0::2][:out_frames]
    odd = activated[1::2][: out_frames - 1]
    taps = [
        jnp.concatenate([first, even[: out_frames - 1]], axis=0),
        jnp.concatenate([first, odd], axis=0),
        even,
    ]
    stacked = jnp.concatenate(taps, axis=-1)
    weights = w_time.reshape(-1, w_time.shape[-1])
    product = jnp.einsum("trwc,cd->trwd", stacked, weights, preferred_element_type=jnp.float32)
    return (product + time_bias).astype(jnp.bfloat16)


def encode_stats(stats):
    high = stats.astype(jnp.bfloat16)
    low = (stats - high.astype(jnp.float32)).astype(jnp.bfloat16)
    return jnp.concatenate([high, low])


def decode_stats(coded, width):
    values = coded.astype(jnp.float32)
    return jnp.sum(values[:, :width], axis=0) + jnp.sum(values[:, width : 2 * width], axis=0)


def shards(clip_frames, frame_of_slot, w_spatial, norm_gain, norm_shift, w_time, time_bias):
    tm_count = lax.axis_size("tm")
    height_count = lax.axis_size("height")
    live_frames = tm_count // 2 + 1
    out_frames = (live_frames - 1) // 2 + 1
    frame_slots = slot_lookup(frame_of_slot, live_frames)
    padded = with_halo(clip_frames, (("height", 1),), 1)
    staged, chan_sums, chan_squares = conv_call(padded[0], w_spatial)
    cols = staged.shape[1] - 1
    own_frame = lax.dynamic_index_in_dim(frame_of_slot, lax.axis_index("tm"), 0, keepdims=False)
    weight = jnp.where(own_frame >= 0, 1.0, 0.0).astype(jnp.float32)
    per_group = staged.shape[-1] // GROUPS
    sums = chan_sums.reshape(GROUPS, per_group).sum(axis=1) * weight
    squares = chan_squares.reshape(GROUPS, per_group).sum(axis=1) * weight
    coded = encode_stats(jnp.concatenate([sums, squares]))
    column = jnp.zeros((staged.shape[-1],), jnp.bfloat16).at[: coded.shape[0]].set(coded)
    payload = staged.at[:, cols, :].set(jnp.broadcast_to(column, (staged.shape[0], column.shape[0])))
    received = lax.all_to_all(payload[None], "tm", split_axis=1, concat_axis=0, tiled=True)
    exchanged = received[:, :, :cols]
    partial = decode_stats(received[:, 0, cols, : coded.shape[0]], 2 * GROUPS)
    other = lax.ppermute(partial, "height", [(0, 1), (1, 0)])
    totals = partial + other
    sums, squares = totals[:GROUPS], totals[GROUPS:]
    cell_count = float(live_frames * clip_frames.shape[1] * height_count * cols * per_group)
    live = jnp.take(exchanged, frame_slots, axis=0)
    activated = normalize(live, sums, squares, cell_count, norm_gain, norm_shift)
    latent = time_conv(activated, w_time, time_bias, out_frames)
    return latent.reshape(out_frames, 1, latent.shape[1], latent.shape[2], latent.shape[3])


def solution(mesh):
    return jax.shard_map(
        shards,
        mesh=mesh,
        in_specs=(P(("dp", "tm"), "height", None, None), P("dp"), P(), P(), P(), P(), P()),
        out_specs=P("dp", "height", "tm", None, None),
        check_vma=False,
    )
```

```python
import functools

import jax
import jax.numpy as jnp
import numpy as np
from jax import lax
from jax.experimental import pallas as pl
from jax.experimental.pallas import tpu as pltpu
from jax.sharding import PartitionSpec as P

GROUPS = 32


def with_halo(block, sides, width):
    for axis, dim in sides:
        count = lax.axis_size(axis)
        forward = [(i, i + 1) for i in range(count - 1)]
        backward = [(target, source) for source, target in forward]
        low = lax.ppermute(
            lax.slice_in_dim(block, block.shape[dim] - width, None, axis=dim), axis, forward
        )
        high = lax.ppermute(lax.slice_in_dim(block, 0, width, axis=dim), axis, backward)
        block = jnp.concatenate([low, block, high], axis=dim)
    return block


def slot_lookup(frame_of_slot, live_frames):
    wanted = jnp.arange(live_frames, dtype=jnp.int32)[:, None]
    places = jnp.arange(frame_of_slot.shape[0], dtype=jnp.int32)[None, :]
    matches = frame_of_slot[None, :] == wanted
    return jnp.sum(jnp.where(matches, places, 0), axis=1)


def conv_kernel(x_ref, w_ref, out_ref, sum_ref, sq_ref, *, chunk, cols):
    step = pl.program_id(0)
    base = step * chunk
    m = chunk * cols
    parts = []
    for col_tap in range(3):
        acc = None
        for row_tap in range(3):
            xs = x_ref[pl.ds(base + row_tap, chunk), :, :].reshape(m, x_ref.shape[-1])
            p = jnp.dot(xs, w_ref[row_tap, col_tap], preferred_element_type=jnp.float32)
            acc = p if acc is None else acc + p
        parts.append(acc)
    col = lax.broadcasted_iota(jnp.int32, (m, 1), 0) % cols
    left = jnp.where(col == 0, 0.0, pltpu.roll(parts[0], 1, 0))
    right = jnp.where(col == cols - 1, 0.0, pltpu.roll(parts[2], m - 1, 0))
    total = (left + parts[1]) + right
    rounded = total.astype(jnp.bfloat16)
    out_ref[:, 0:cols, :] = rounded.reshape(chunk, cols, -1)
    out_ref[:, cols:cols + 1, :] = jnp.zeros((chunk, 1, out_ref.shape[-1]), jnp.bfloat16)
    values = rounded.astype(jnp.float32)

    @pl.when(step == 0)
    def _():
        sum_ref[...] = jnp.zeros_like(sum_ref)
        sq_ref[...] = jnp.zeros_like(sq_ref)

    sum_ref[...] += jnp.sum(values, axis=0, keepdims=True)
    sq_ref[...] += jnp.sum(values * values, axis=0, keepdims=True)

def conv_call(x, w, chunk=8):
    rows = x.shape[0] - 2
    cols = x.shape[1]
    cin = x.shape[2]
    cout = w.shape[-1]
    return pl.pallas_call(
        functools.partial(conv_kernel, chunk=chunk, cols=cols),
        grid=(rows // chunk,),
        in_specs=[
            pl.BlockSpec((rows + 2, cols, cin), lambda i: (0, 0, 0)),
            pl.BlockSpec((3, 3, cin, cout), lambda i: (0, 0, 0, 0)),
        ],
        out_specs=[
            pl.BlockSpec((chunk, cols + 1, cout), lambda i: (i, 0, 0)),
            pl.BlockSpec((1, cout), lambda i: (0, 0)),
            pl.BlockSpec((1, cout), lambda i: (0, 0)),
        ],
        out_shape=[
            jax.ShapeDtypeStruct((rows, cols + 1, cout), jnp.bfloat16),
            jax.ShapeDtypeStruct((1, cout), jnp.float32),
            jax.ShapeDtypeStruct((1, cout), jnp.float32),
        ],
        compiler_params=pltpu.CompilerParams(dimension_semantics=("arbitrary",)),
    )(x, w)


def latent_kernel(slots_ref, x0_ref, x1_ref, x2_ref, w_ref, mean_ref, scale_ref, gain_ref, shift_ref, bias_ref, out_ref):
    running = bias_ref[...]
    for time_tap, x_ref in enumerate((x0_ref, x1_ref, x2_ref)):
        values = x_ref[0].astype(jnp.float32)
        normed = (values - mean_ref[...]) * scale_ref[...] * gain_ref[...] + shift_ref[...]
        activated = jax.nn.silu(normed).astype(jnp.bfloat16)
        running = running + jnp.dot(activated, w_ref[time_tap], preferred_element_type=jnp.float32)
    out_ref[0] = running.astype(jnp.bfloat16)


def tap_spec(time_tap, cols, chans):
    def index(step, slots):
        return (slots[jnp.maximum(2 * step + time_tap - 2, 0)], 0, 0)

    return pl.BlockSpec((1, cols, chans), index)


def latent_call(frame_slots, received, w_time, mean_chan, scale_chan, norm_gain, norm_shift, time_bias, out_frames, cols):
    chans = received.shape[-1]
    vec = pl.BlockSpec((1, chans), lambda step, slots: (0, 0))
    grid_spec = pltpu.PrefetchScalarGridSpec(
        num_scalar_prefetch=1,
        grid=(out_frames,),
        in_specs=[
            tap_spec(0, cols, chans),
            tap_spec(1, cols, chans),
            tap_spec(2, cols, chans),
            pl.BlockSpec(w_time.shape, lambda step, slots: (0, 0, 0)),
            vec, vec, vec, vec, vec,
        ],
        out_specs=pl.BlockSpec((1, cols, chans), lambda step, slots: (step, 0, 0)),
    )
    row = lambda v: v.reshape(1, chans).astype(jnp.float32)
    return pl.pallas_call(
        latent_kernel,
        grid_spec=grid_spec,
        out_shape=jax.ShapeDtypeStruct((out_frames, cols, chans), jnp.bfloat16),
        compiler_params=pltpu.CompilerParams(dimension_semantics=("arbitrary",)),
    )(
        frame_slots, received, received, received, w_time,
        row(mean_chan), row(scale_chan), row(norm_gain), row(norm_shift), row(time_bias),
    )


def spatial_conv(row_padded, w_spatial):
    out = lax.conv_general_dilated(
        row_padded,
        w_spatial,
        window_strides=(1, 1),
        padding=((0, 0), (1, 1)),
        dimension_numbers=("NHWC", "HWIO", "NHWC"),
        preferred_element_type=jnp.float32,
    )
    return out.astype(jnp.bfloat16)


def group_stats(conv_out, weight):
    cout_width = conv_out.shape[-1]
    per_group = cout_width // GROUPS
    values = conv_out.astype(jnp.float32).reshape(-1, cout_width)
    sums = jnp.sum(values, axis=0).reshape(GROUPS, per_group).sum(axis=1) * weight
    squares = jnp.sum(values * values, axis=0).reshape(GROUPS, per_group).sum(axis=1) * weight
    return sums, squares


def normalize(conv_out, sums, squares, cell_count, norm_gain, norm_shift):
    per_group = conv_out.shape[-1] // GROUPS
    group_mean = sums / cell_count
    group_var = squares / cell_count - group_mean * group_mean
    inv_scale = lax.rsqrt(group_var + 1e-06)
    mean_chan = jnp.repeat(group_mean, per_group)
    scale_chan = jnp.repeat(inv_scale, per_group)
    values = conv_out.astype(jnp.float32)
    return jax.nn.silu((values - mean_chan) * scale_chan * norm_gain + norm_shift).astype(
        jnp.bfloat16
    )


def time_conv(activated, w_time, time_bias, out_frames):
    first = activated[0:1]
    even = activated[0::2][:out_frames]
    odd = activated[1::2][: out_frames - 1]
    taps = [
        jnp.concatenate([first, even[: out_frames - 1]], axis=0),
        jnp.concatenate([first, odd], axis=0),
        even,
    ]
    stacked = jnp.concatenate(taps, axis=-1)
    weights = w_time.reshape(-1, w_time.shape[-1])
    product = jnp.einsum("trwc,cd->trwd", stacked, weights, preferred_element_type=jnp.float32)
    return (product + time_bias).astype(jnp.bfloat16)


def encode_stats(stats):
    high = stats.astype(jnp.bfloat16)
    low = (stats - high.astype(jnp.float32)).astype(jnp.bfloat16)
    return jnp.concatenate([high, low])


def decode_stats(coded, width):
    values = coded.astype(jnp.float32)
    return jnp.sum(values[:, :width], axis=0) + jnp.sum(values[:, width : 2 * width], axis=0)


def shards(clip_frames, frame_of_slot, w_spatial, norm_gain, norm_shift, w_time, time_bias):
    tm_count = lax.axis_size("tm")
    height_count = lax.axis_size("height")
    live_frames = tm_count // 2 + 1
    out_frames = (live_frames - 1) // 2 + 1
    frame_slots = slot_lookup(frame_of_slot, live_frames)
    padded = with_halo(clip_frames, (("height", 1),), 1)
    staged, chan_sums, chan_squares = conv_call(padded[0], w_spatial)
    cols = staged.shape[1] - 1
    own_frame = lax.dynamic_index_in_dim(frame_of_slot, lax.axis_index("tm"), 0, keepdims=False)
    weight = jnp.where(own_frame >= 0, 1.0, 0.0).astype(jnp.float32)
    per_group = staged.shape[-1] // GROUPS
    sums = chan_sums.reshape(GROUPS, per_group).sum(axis=1) * weight
    squares = chan_squares.reshape(GROUPS, per_group).sum(axis=1) * weight
    coded = encode_stats(jnp.concatenate([sums, squares]))
    column = jnp.zeros((staged.shape[-1],), jnp.bfloat16).at[: coded.shape[0]].set(coded)
    payload = staged.at[:, cols, :].set(jnp.broadcast_to(column, (staged.shape[0], column.shape[0])))
    received = lax.all_to_all(payload[None], "tm", split_axis=1, concat_axis=0, tiled=True)
    partial = decode_stats(received[:, 0, cols, : coded.shape[0]], 2 * GROUPS)
    other = lax.ppermute(partial, "height", [(0, 1), (1, 0)])
    totals = partial + other
    sums, squares = totals[:GROUPS], totals[GROUPS:]
    cell_count = float(live_frames * clip_frames.shape[1] * height_count * cols * per_group)
    group_mean = sums / cell_count
    group_var = squares / cell_count - group_mean * group_mean
    inv_scale = lax.rsqrt(group_var + 1e-06)
    latent = latent_call(
        frame_slots.astype(jnp.int32),
        received[0] if received.ndim == 3 else received.reshape(received.shape[0], cols + 1, -1),
        w_time,
        jnp.repeat(group_mean, per_group),
        jnp.repeat(inv_scale, per_group),
        norm_gain,
        norm_shift,
        time_bias,
        out_frames,
        cols,
    )
    latent = latent.reshape(out_frames, 1, cols, latent.shape[-1])
    return latent.reshape(out_frames, 1, latent.shape[1], latent.shape[2], latent.shape[3])


def solution(mesh):
    return jax.shard_map(
        shards,
        mesh=mesh,
        in_specs=(P(("dp", "tm"), "height", None, None), P("dp"), P(), P(), P(), P(), P()),
        out_specs=P("dp", "height", "tm", None, None),
        check_vma=False,
    )
```

```python
import functools

import jax
import jax.numpy as jnp
import numpy as np
from jax import lax
from jax.experimental import pallas as pl
from jax.experimental.pallas import tpu as pltpu
from jax.sharding import PartitionSpec as P

GROUPS = 32


def with_halo(block, sides, width):
    for axis, dim in sides:
        count = lax.axis_size(axis)
        forward = [(i, i + 1) for i in range(count - 1)]
        backward = [(target, source) for source, target in forward]
        low = lax.ppermute(
            lax.slice_in_dim(block, block.shape[dim] - width, None, axis=dim), axis, forward
        )
        high = lax.ppermute(lax.slice_in_dim(block, 0, width, axis=dim), axis, backward)
        block = jnp.concatenate([low, block, high], axis=dim)
    return block


def slot_lookup(frame_of_slot, live_frames):
    wanted = jnp.arange(live_frames, dtype=jnp.int32)[:, None]
    places = jnp.arange(frame_of_slot.shape[0], dtype=jnp.int32)[None, :]
    matches = frame_of_slot[None, :] == wanted
    return jnp.sum(jnp.where(matches, places, 0), axis=1)


def conv_kernel(x_ref, w_ref, out_ref, sum_ref, sq_ref, *, chunk, cols):
    step = pl.program_id(0)
    base = step * chunk
    m = chunk * cols
    parts = []
    for col_tap in range(3):
        acc = None
        for row_tap in range(3):
            xs = x_ref[pl.ds(base + row_tap, chunk), :, :].reshape(m, x_ref.shape[-1])
            p = jnp.dot(xs, w_ref[row_tap, col_tap], preferred_element_type=jnp.float32)
            acc = p if acc is None else acc + p
        parts.append(acc)
    col = lax.broadcasted_iota(jnp.int32, (m, 1), 0) % cols
    left = jnp.where(col == 0, 0.0, pltpu.roll(parts[0], 1, 0))
    right = jnp.where(col == cols - 1, 0.0, pltpu.roll(parts[2], m - 1, 0))
    total = (left + parts[1]) + right
    rounded = total.astype(jnp.bfloat16)
    out_ref[:, 0:cols, :] = rounded.reshape(chunk, cols, -1)
    out_ref[:, cols:cols + 1, :] = jnp.zeros((chunk, 1, out_ref.shape[-1]), jnp.bfloat16)
    values = rounded.astype(jnp.float32)

    @pl.when(step == 0)
    def _():
        sum_ref[...] = jnp.zeros_like(sum_ref)
        sq_ref[...] = jnp.zeros_like(sq_ref)

    sum_ref[...] += jnp.sum(values, axis=0, keepdims=True)
    sq_ref[...] += jnp.sum(values * values, axis=0, keepdims=True)

def conv_call(x, w, chunk=8):
    rows = x.shape[0] - 2
    cols = x.shape[1]
    cin = x.shape[2]
    cout = w.shape[-1]
    return pl.pallas_call(
        functools.partial(conv_kernel, chunk=chunk, cols=cols),
        grid=(rows // chunk,),
        in_specs=[
            pl.BlockSpec((rows + 2, cols, cin), lambda i: (0, 0, 0)),
            pl.BlockSpec((3, 3, cin, cout), lambda i: (0, 0, 0, 0)),
        ],
        out_specs=[
            pl.BlockSpec((chunk, cols + 1, cout), lambda i: (i, 0, 0)),
            pl.BlockSpec((1, cout), lambda i: (0, 0)),
            pl.BlockSpec((1, cout), lambda i: (0, 0)),
        ],
        out_shape=[
            jax.ShapeDtypeStruct((rows, cols + 1, cout), jnp.bfloat16),
            jax.ShapeDtypeStruct((1, cout), jnp.float32),
            jax.ShapeDtypeStruct((1, cout), jnp.float32),
        ],
        compiler_params=pltpu.CompilerParams(dimension_semantics=("arbitrary",)),
    )(x, w)


def latent_kernel(slots_ref, x1_ref, x2_ref, w_ref, mean_ref, scale_ref, gain_ref, shift_ref, bias_ref, out_ref, prev_ref):
    def activate(x_ref):
        values = x_ref[0].astype(jnp.float32)
        normed = (values - mean_ref[...]) * scale_ref[...] * gain_ref[...] + shift_ref[...]
        return jax.nn.silu(normed).astype(jnp.bfloat16)

    odd = activate(x1_ref)
    even = activate(x2_ref)

    @pl.when(pl.program_id(0) == 0)
    def _():
        prev_ref[...] = even

    running = bias_ref[...]
    running = running + jnp.dot(prev_ref[...], w_ref[0], preferred_element_type=jnp.float32)
    running = running + jnp.dot(odd, w_ref[1], preferred_element_type=jnp.float32)
    running = running + jnp.dot(even, w_ref[2], preferred_element_type=jnp.float32)
    out_ref[0] = running.astype(jnp.bfloat16)
    prev_ref[...] = even


def tap_spec(time_tap, cols, chans):
    def index(step, slots):
        return (slots[jnp.maximum(2 * step + time_tap - 2, 0)], 0, 0)

    return pl.BlockSpec((1, cols, chans), index)


def latent_call(frame_slots, received, w_time, mean_chan, scale_chan, norm_gain, norm_shift, time_bias, out_frames, cols):
    chans = received.shape[-1]
    vec = pl.BlockSpec((1, chans), lambda step, slots: (0, 0))
    grid_spec = pltpu.PrefetchScalarGridSpec(
        num_scalar_prefetch=1,
        grid=(out_frames,),
        in_specs=[
            tap_spec(1, cols, chans),
            tap_spec(2, cols, chans),
            pl.BlockSpec(w_time.shape, lambda step, slots: (0, 0, 0)),
            vec, vec, vec, vec, vec,
        ],
        out_specs=pl.BlockSpec((1, cols, chans), lambda step, slots: (step, 0, 0)),
        scratch_shapes=[pltpu.VMEM((cols, chans), jnp.bfloat16)],
    )
    row = lambda v: v.reshape(1, chans).astype(jnp.float32)
    return pl.pallas_call(
        latent_kernel,
        grid_spec=grid_spec,
        out_shape=jax.ShapeDtypeStruct((out_frames, cols, chans), jnp.bfloat16),
        compiler_params=pltpu.CompilerParams(dimension_semantics=("arbitrary",)),
    )(
        frame_slots, received, received, w_time,
        row(mean_chan), row(scale_chan), row(norm_gain), row(norm_shift), row(time_bias),
    )


def spatial_conv(row_padded, w_spatial):
    out = lax.conv_general_dilated(
        row_padded,
        w_spatial,
        window_strides=(1, 1),
        padding=((0, 0), (1, 1)),
        dimension_numbers=("NHWC", "HWIO", "NHWC"),
        preferred_element_type=jnp.float32,
    )
    return out.astype(jnp.bfloat16)


def group_stats(conv_out, weight):
    cout_width = conv_out.shape[-1]
    per_group = cout_width // GROUPS
    values = conv_out.astype(jnp.float32).reshape(-1, cout_width)
    sums = jnp.sum(values, axis=0).reshape(GROUPS, per_group).sum(axis=1) * weight
    squares = jnp.sum(values * values, axis=0).reshape(GROUPS, per_group).sum(axis=1) * weight
    return sums, squares


def normalize(conv_out, sums, squares, cell_count, norm_gain, norm_shift):
    per_group = conv_out.shape[-1] // GROUPS
    group_mean = sums / cell_count
    group_var = squares / cell_count - group_mean * group_mean
    inv_scale = lax.rsqrt(group_var + 1e-06)
    mean_chan = jnp.repeat(group_mean, per_group)
    scale_chan = jnp.repeat(inv_scale, per_group)
    values = conv_out.astype(jnp.float32)
    return jax.nn.silu((values - mean_chan) * scale_chan * norm_gain + norm_shift).astype(
        jnp.bfloat16
    )


def time_conv(activated, w_time, time_bias, out_frames):
    first = activated[0:1]
    even = activated[0::2][:out_frames]
    odd = activated[1::2][: out_frames - 1]
    taps = [
        jnp.concatenate([first, even[: out_frames - 1]], axis=0),
        jnp.concatenate([first, odd], axis=0),
        even,
    ]
    stacked = jnp.concatenate(taps, axis=-1)
    weights = w_time.reshape(-1, w_time.shape[-1])
    product = jnp.einsum("trwc,cd->trwd", stacked, weights, preferred_element_type=jnp.float32)
    return (product + time_bias).astype(jnp.bfloat16)


def encode_stats(stats):
    high = stats.astype(jnp.bfloat16)
    low = (stats - high.astype(jnp.float32)).astype(jnp.bfloat16)
    return jnp.concatenate([high, low])


def decode_stats(coded, width):
    values = coded.astype(jnp.float32)
    return jnp.sum(values[:, :width], axis=0) + jnp.sum(values[:, width : 2 * width], axis=0)


def shards(clip_frames, frame_of_slot, w_spatial, norm_gain, norm_shift, w_time, time_bias):
    tm_count = lax.axis_size("tm")
    height_count = lax.axis_size("height")
    live_frames = tm_count // 2 + 1
    out_frames = (live_frames - 1) // 2 + 1
    frame_slots = slot_lookup(frame_of_slot, live_frames)
    padded = with_halo(clip_frames, (("height", 1),), 1)
    staged, chan_sums, chan_squares = conv_call(padded[0], w_spatial)
    cols = staged.shape[1] - 1
    own_frame = lax.dynamic_index_in_dim(frame_of_slot, lax.axis_index("tm"), 0, keepdims=False)
    weight = jnp.where(own_frame >= 0, 1.0, 0.0).astype(jnp.float32)
    per_group = staged.shape[-1] // GROUPS
    sums = chan_sums.reshape(GROUPS, per_group).sum(axis=1) * weight
    squares = chan_squares.reshape(GROUPS, per_group).sum(axis=1) * weight
    coded = encode_stats(jnp.concatenate([sums, squares]))
    column = jnp.zeros((staged.shape[-1],), jnp.bfloat16).at[: coded.shape[0]].set(coded)
    payload = staged.at[:, cols, :].set(jnp.broadcast_to(column, (staged.shape[0], column.shape[0])))
    received = lax.all_to_all(payload[None], "tm", split_axis=1, concat_axis=0, tiled=True)
    partial = decode_stats(received[:, 0, cols, : coded.shape[0]], 2 * GROUPS)
    other = lax.ppermute(partial, "height", [(0, 1), (1, 0)])
    totals = partial + other
    sums, squares = totals[:GROUPS], totals[GROUPS:]
    cell_count = float(live_frames * clip_frames.shape[1] * height_count * cols * per_group)
    group_mean = sums / cell_count
    group_var = squares / cell_count - group_mean * group_mean
    inv_scale = lax.rsqrt(group_var + 1e-06)
    latent = latent_call(
        frame_slots.astype(jnp.int32),
        received[0] if received.ndim == 3 else received.reshape(received.shape[0], cols + 1, -1),
        w_time,
        jnp.repeat(group_mean, per_group),
        jnp.repeat(inv_scale, per_group),
        norm_gain,
        norm_shift,
        time_bias,
        out_frames,
        cols,
    )
    latent = latent.reshape(out_frames, 1, cols, latent.shape[-1])
    return latent.reshape(out_frames, 1, latent.shape[1], latent.shape[2], latent.shape[3])


def solution(mesh):
    return jax.shard_map(
        shards,
        mesh=mesh,
        in_specs=(P(("dp", "tm"), "height", None, None), P("dp"), P(), P(), P(), P(), P()),
        out_specs=P("dp", "height", "tm", None, None),
        check_vma=False,
    )
```

```python
import functools

import jax
import jax.numpy as jnp
import numpy as np
from jax import lax
from jax.experimental import pallas as pl
from jax.experimental.pallas import tpu as pltpu
from jax.sharding import PartitionSpec as P

GROUPS = 32


def with_halo(block, sides, width):
    for axis, dim in sides:
        count = lax.axis_size(axis)
        forward = [(i, i + 1) for i in range(count - 1)]
        backward = [(target, source) for source, target in forward]
        low = lax.ppermute(
            lax.slice_in_dim(block, block.shape[dim] - width, None, axis=dim), axis, forward
        )
        high = lax.ppermute(lax.slice_in_dim(block, 0, width, axis=dim), axis, backward)
        block = jnp.concatenate([low, block, high], axis=dim)
    return block


def slot_lookup(frame_of_slot, live_frames):
    wanted = jnp.arange(live_frames, dtype=jnp.int32)[:, None]
    places = jnp.arange(frame_of_slot.shape[0], dtype=jnp.int32)[None, :]
    matches = frame_of_slot[None, :] == wanted
    return jnp.sum(jnp.where(matches, places, 0), axis=1)


def conv_kernel(x_ref, w_ref, out_ref, sum_ref, sq_ref, *, chunk, cols):
    step = pl.program_id(0)
    base = step * chunk
    m = chunk * cols
    parts = []
    for col_tap in range(3):
        acc = None
        for row_tap in range(3):
            xs = x_ref[pl.ds(base + row_tap, chunk), :, :].reshape(m, x_ref.shape[-1])
            p = jnp.dot(xs, w_ref[row_tap, col_tap], preferred_element_type=jnp.float32)
            acc = p if acc is None else acc + p
        parts.append(acc)
    col = lax.broadcasted_iota(jnp.int32, (m, 1), 0) % cols
    left = jnp.where(col == 0, 0.0, pltpu.roll(parts[0], 1, 0))
    right = jnp.where(col == cols - 1, 0.0, pltpu.roll(parts[2], m - 1, 0))
    total = (left + parts[1]) + right
    rounded = total.astype(jnp.bfloat16)
    out_ref[:, 0:cols, :] = rounded.reshape(chunk, cols, -1)
    out_ref[:, cols:cols + 1, :] = jnp.zeros((chunk, 1, out_ref.shape[-1]), jnp.bfloat16)
    values = rounded.astype(jnp.float32)

    @pl.when(step == 0)
    def _():
        sum_ref[...] = jnp.zeros_like(sum_ref)
        sq_ref[...] = jnp.zeros_like(sq_ref)

    sum_ref[...] += jnp.sum(values, axis=0, keepdims=True)
    sq_ref[...] += jnp.sum(values * values, axis=0, keepdims=True)

def conv_call(x, w, chunk=8):
    rows = x.shape[0] - 2
    cols = x.shape[1]
    cin = x.shape[2]
    cout = w.shape[-1]
    return pl.pallas_call(
        functools.partial(conv_kernel, chunk=chunk, cols=cols),
        grid=(rows // chunk,),
        in_specs=[
            pl.BlockSpec((rows + 2, cols, cin), lambda i: (0, 0, 0)),
            pl.BlockSpec((3, 3, cin, cout), lambda i: (0, 0, 0, 0)),
        ],
        out_specs=[
            pl.BlockSpec((chunk, cols + 1, cout), lambda i: (i, 0, 0)),
            pl.BlockSpec((1, cout), lambda i: (0, 0)),
            pl.BlockSpec((1, cout), lambda i: (0, 0)),
        ],
        out_shape=[
            jax.ShapeDtypeStruct((rows, cols + 1, cout), jnp.bfloat16),
            jax.ShapeDtypeStruct((1, cout), jnp.float32),
            jax.ShapeDtypeStruct((1, cout), jnp.float32),
        ],
        compiler_params=pltpu.CompilerParams(dimension_semantics=("arbitrary",)),
    )(x, w)


def latent_kernel(slots_ref, x_ref, w_ref, mean_ref, scale_ref, gain_ref, shift_ref, bias_ref, out_ref, tap0_ref, tap1_ref, tap2_ref):
    live = 2 * out_ref.shape[0] - 1
    cols, chans = out_ref.shape[1], out_ref.shape[2]
    for frame in range(live):
        values = x_ref[slots_ref[frame], pl.ds(0, cols), :].astype(jnp.float32)
        normed = (values - mean_ref[...]) * scale_ref[...] * gain_ref[...] + shift_ref[...]
        activated = jax.nn.silu(normed).astype(jnp.bfloat16)
        if frame == 0:
            tap0_ref[0] = activated
            tap1_ref[0] = activated
        if frame % 2 == 0:
            tap2_ref[frame // 2] = activated
            if frame // 2 + 1 < out_ref.shape[0]:
                tap0_ref[frame // 2 + 1] = activated
        else:
            tap1_ref[(frame + 1) // 2] = activated
    rows = out_ref.shape[0] * cols
    running = bias_ref[...]
    for time_tap, tap_ref in enumerate((tap0_ref, tap1_ref, tap2_ref)):
        block = tap_ref[...].reshape(rows, chans)
        running = running + jnp.dot(block, w_ref[time_tap], preferred_element_type=jnp.float32)
    out_ref[...] = running.astype(jnp.bfloat16).reshape(out_ref.shape)


def latent_call(frame_slots, received, w_time, mean_chan, scale_chan, norm_gain, norm_shift, time_bias, out_frames, cols):
    chans = received.shape[-1]
    vmem = pltpu.MemorySpace.VMEM if hasattr(pltpu, "MemorySpace") else pltpu.TPUMemorySpace.VMEM
    smem = pltpu.MemorySpace.SMEM if hasattr(pltpu, "MemorySpace") else pltpu.TPUMemorySpace.SMEM
    row = lambda v: v.reshape(1, chans).astype(jnp.float32)
    tap = pltpu.VMEM((out_frames, cols, chans), jnp.bfloat16)
    return pl.pallas_call(
        latent_kernel,
        in_specs=[pl.BlockSpec(memory_space=smem)] + [pl.BlockSpec(memory_space=vmem)] * 7,
        out_specs=pl.BlockSpec(memory_space=vmem),
        out_shape=jax.ShapeDtypeStruct((out_frames, cols, chans), jnp.bfloat16),
        scratch_shapes=[tap, tap, tap],
    )(
        frame_slots, received, w_time,
        row(mean_chan), row(scale_chan), row(norm_gain), row(norm_shift), row(time_bias),
    )

def spatial_conv(row_padded, w_spatial):
    out = lax.conv_general_dilated(
        row_padded,
        w_spatial,
        window_strides=(1, 1),
        padding=((0, 0), (1, 1)),
        dimension_numbers=("NHWC", "HWIO", "NHWC"),
        preferred_element_type=jnp.float32,
    )
    return out.astype(jnp.bfloat16)


def group_stats(conv_out, weight):
    cout_width = conv_out.shape[-1]
    per_group = cout_width // GROUPS
    values = conv_out.astype(jnp.float32).reshape(-1, cout_width)
    sums = jnp.sum(values, axis=0).reshape(GROUPS, per_group).sum(axis=1) * weight
    squares = jnp.sum(values * values, axis=0).reshape(GROUPS, per_group).sum(axis=1) * weight
    return sums, squares


def normalize(conv_out, sums, squares, cell_count, norm_gain, norm_shift):
    per_group = conv_out.shape[-1] // GROUPS
    group_mean = sums / cell_count
    group_var = squares / cell_count - group_mean * group_mean
    inv_scale = lax.rsqrt(group_var + 1e-06)
    mean_chan = jnp.repeat(group_mean, per_group)
    scale_chan = jnp.repeat(inv_scale, per_group)
    values = conv_out.astype(jnp.float32)
    return jax.nn.silu((values - mean_chan) * scale_chan * norm_gain + norm_shift).astype(
        jnp.bfloat16
    )


def time_conv(activated, w_time, time_bias, out_frames):
    first = activated[0:1]
    even = activated[0::2][:out_frames]
    odd = activated[1::2][: out_frames - 1]
    taps = [
        jnp.concatenate([first, even[: out_frames - 1]], axis=0),
        jnp.concatenate([first, odd], axis=0),
        even,
    ]
    stacked = jnp.concatenate(taps, axis=-1)
    weights = w_time.reshape(-1, w_time.shape[-1])
    product = jnp.einsum("trwc,cd->trwd", stacked, weights, preferred_element_type=jnp.float32)
    return (product + time_bias).astype(jnp.bfloat16)


def encode_stats(stats):
    high = stats.astype(jnp.bfloat16)
    low = (stats - high.astype(jnp.float32)).astype(jnp.bfloat16)
    return jnp.concatenate([high, low])


def decode_stats(coded, width):
    values = coded.astype(jnp.float32)
    return jnp.sum(values[:, :width], axis=0) + jnp.sum(values[:, width : 2 * width], axis=0)


def shards(clip_frames, frame_of_slot, w_spatial, norm_gain, norm_shift, w_time, time_bias):
    tm_count = lax.axis_size("tm")
    height_count = lax.axis_size("height")
    live_frames = tm_count // 2 + 1
    out_frames = (live_frames - 1) // 2 + 1
    frame_slots = slot_lookup(frame_of_slot, live_frames)
    padded = with_halo(clip_frames, (("height", 1),), 1)
    staged, chan_sums, chan_squares = conv_call(padded[0], w_spatial)
    cols = staged.shape[1] - 1
    own_frame = lax.dynamic_index_in_dim(frame_of_slot, lax.axis_index("tm"), 0, keepdims=False)
    weight = jnp.where(own_frame >= 0, 1.0, 0.0).astype(jnp.float32)
    per_group = staged.shape[-1] // GROUPS
    sums = chan_sums.reshape(GROUPS, per_group).sum(axis=1) * weight
    squares = chan_squares.reshape(GROUPS, per_group).sum(axis=1) * weight
    coded = encode_stats(jnp.concatenate([sums, squares]))
    column = jnp.zeros((staged.shape[-1],), jnp.bfloat16).at[: coded.shape[0]].set(coded)
    payload = staged.at[:, cols, :].set(jnp.broadcast_to(column, (staged.shape[0], column.shape[0])))
    received = lax.all_to_all(payload[None], "tm", split_axis=1, concat_axis=0, tiled=True)
    partial = decode_stats(received[:, 0, cols, : coded.shape[0]], 2 * GROUPS)
    other = lax.ppermute(partial, "height", [(0, 1), (1, 0)])
    totals = partial + other
    sums, squares = totals[:GROUPS], totals[GROUPS:]
    cell_count = float(live_frames * clip_frames.shape[1] * height_count * cols * per_group)
    group_mean = sums / cell_count
    group_var = squares / cell_count - group_mean * group_mean
    inv_scale = lax.rsqrt(group_var + 1e-06)
    latent = latent_call(
        frame_slots.astype(jnp.int32),
        received.reshape(received.shape[0], cols + 1, -1),
        w_time,
        jnp.repeat(group_mean, per_group),
        jnp.repeat(inv_scale, per_group),
        norm_gain,
        norm_shift,
        time_bias,
        out_frames,
        cols,
    )
    latent = latent.reshape(out_frames, 1, cols, latent.shape[-1])
    return latent.reshape(out_frames, 1, latent.shape[1], latent.shape[2], latent.shape[3])


def solution(mesh):
    return jax.shard_map(
        shards,
        mesh=mesh,
        in_specs=(P(("dp", "tm"), "height", None, None), P("dp"), P(), P(), P(), P(), P()),
        out_specs=P("dp", "height", "tm", None, None),
        check_vma=False,
    )
```

```python
import functools

import jax
import jax.numpy as jnp
import numpy as np
from jax import lax
from jax.experimental import pallas as pl
from jax.experimental.pallas import tpu as pltpu
from jax.sharding import PartitionSpec as P

GROUPS = 32


def with_halo(block, sides, width):
    for axis, dim in sides:
        count = lax.axis_size(axis)
        forward = [(i, i + 1) for i in range(count - 1)]
        backward = [(target, source) for source, target in forward]
        low = lax.ppermute(
            lax.slice_in_dim(block, block.shape[dim] - width, None, axis=dim), axis, forward
        )
        high = lax.ppermute(lax.slice_in_dim(block, 0, width, axis=dim), axis, backward)
        block = jnp.concatenate([low, block, high], axis=dim)
    return block


def slot_lookup(frame_of_slot, live_frames):
    wanted = jnp.arange(live_frames, dtype=jnp.int32)[:, None]
    places = jnp.arange(frame_of_slot.shape[0], dtype=jnp.int32)[None, :]
    matches = frame_of_slot[None, :] == wanted
    return jnp.sum(jnp.where(matches, places, 0), axis=1)


def conv_kernel(x_ref, w_ref, out_ref, sum_ref, sq_ref, *, chunk, cols):
    step = pl.program_id(0)
    base = step * chunk
    m = chunk * cols
    parts = []
    for col_tap in range(3):
        acc = None
        for row_tap in range(3):
            xs = x_ref[pl.ds(base + row_tap, chunk), :, :].reshape(m, x_ref.shape[-1])
            p = jnp.dot(xs, w_ref[row_tap, col_tap], preferred_element_type=jnp.float32)
            acc = p if acc is None else acc + p
        parts.append(acc)
    col = lax.broadcasted_iota(jnp.int32, (m, 1), 0) % cols
    left = jnp.where(col == 0, 0.0, pltpu.roll(parts[0], 1, 0))
    right = jnp.where(col == cols - 1, 0.0, pltpu.roll(parts[2], m - 1, 0))
    total = (left + parts[1]) + right
    rounded = total.astype(jnp.bfloat16)
    lanes = out_ref.shape[-1]
    for quarter in range(rounded.shape[-1] // lanes):
        piece = rounded[:, quarter * lanes : (quarter + 1) * lanes]
        out_ref[:, quarter * cols : (quarter + 1) * cols, :] = piece.reshape(chunk, cols, lanes)
    tail = out_ref.shape[1] - 1
    out_ref[:, tail : tail + 1, :] = jnp.zeros((chunk, 1, lanes), jnp.bfloat16)
    values = rounded.astype(jnp.float32)

    @pl.when(step == 0)
    def _():
        sum_ref[...] = jnp.zeros_like(sum_ref)
        sq_ref[...] = jnp.zeros_like(sq_ref)

    sum_ref[...] += jnp.sum(values, axis=0, keepdims=True)
    sq_ref[...] += jnp.sum(values * values, axis=0, keepdims=True)

def conv_call(x, w, chunk=8, lanes=128):
    rows = x.shape[0] - 2
    cols = x.shape[1]
    cin = x.shape[2]
    cout = w.shape[-1]
    stacked = cols * (cout // lanes) + 1
    return pl.pallas_call(
        functools.partial(conv_kernel, chunk=chunk, cols=cols),
        grid=(rows // chunk,),
        in_specs=[
            pl.BlockSpec((rows + 2, cols, cin), lambda i: (0, 0, 0)),
            pl.BlockSpec((3, 3, cin, cout), lambda i: (0, 0, 0, 0)),
        ],
        out_specs=[
            pl.BlockSpec((chunk, stacked, lanes), lambda i: (i, 0, 0)),
            pl.BlockSpec((1, cout), lambda i: (0, 0)),
            pl.BlockSpec((1, cout), lambda i: (0, 0)),
        ],
        out_shape=[
            jax.ShapeDtypeStruct((rows, stacked, lanes), jnp.bfloat16),
            jax.ShapeDtypeStruct((1, cout), jnp.float32),
            jax.ShapeDtypeStruct((1, cout), jnp.float32),
        ],
        compiler_params=pltpu.CompilerParams(dimension_semantics=("arbitrary",)),
    )(x, w)


def latent_kernel(slots_ref, x_ref, w_ref, mean_ref, scale_ref, gain_ref, shift_ref, bias_ref, out_ref, tap0_ref, tap1_ref, tap2_ref):
    live = 2 * out_ref.shape[0] - 1
    cols, chans = out_ref.shape[1], out_ref.shape[2]
    for frame in range(live):
        slot = slots_ref[frame]
        lanes = x_ref.shape[-1]
        pieces = [x_ref[slot, pl.ds(q * cols, cols), :] for q in range(chans // lanes)]
        values = jnp.concatenate(pieces, axis=-1).astype(jnp.float32)
        normed = (values - mean_ref[...]) * scale_ref[...] * gain_ref[...] + shift_ref[...]
        activated = jax.nn.silu(normed).astype(jnp.bfloat16)
        if frame == 0:
            tap0_ref[0] = activated
            tap1_ref[0] = activated
        if frame % 2 == 0:
            tap2_ref[frame // 2] = activated
            if frame // 2 + 1 < out_ref.shape[0]:
                tap0_ref[frame // 2 + 1] = activated
        else:
            tap1_ref[(frame + 1) // 2] = activated
    rows = out_ref.shape[0] * cols
    running = bias_ref[...]
    for time_tap, tap_ref in enumerate((tap0_ref, tap1_ref, tap2_ref)):
        block = tap_ref[...].reshape(rows, chans)
        running = running + jnp.dot(block, w_ref[time_tap], preferred_element_type=jnp.float32)
    out_ref[...] = running.astype(jnp.bfloat16).reshape(out_ref.shape)


def latent_call(frame_slots, received, w_time, mean_chan, scale_chan, norm_gain, norm_shift, time_bias, out_frames, cols):
    chans = w_time.shape[-1]
    vmem = pltpu.MemorySpace.VMEM if hasattr(pltpu, "MemorySpace") else pltpu.TPUMemorySpace.VMEM
    smem = pltpu.MemorySpace.SMEM if hasattr(pltpu, "MemorySpace") else pltpu.TPUMemorySpace.SMEM
    row = lambda v: v.reshape(1, chans).astype(jnp.float32)
    tap = pltpu.VMEM((out_frames, cols, chans), jnp.bfloat16)
    return pl.pallas_call(
        latent_kernel,
        in_specs=[pl.BlockSpec(memory_space=smem)] + [pl.BlockSpec(memory_space=vmem)] * 7,
        out_specs=pl.BlockSpec(memory_space=vmem),
        out_shape=jax.ShapeDtypeStruct((out_frames, cols, chans), jnp.bfloat16),
        scratch_shapes=[tap, tap, tap],
    )(
        frame_slots, received, w_time,
        row(mean_chan), row(scale_chan), row(norm_gain), row(norm_shift), row(time_bias),
    )

def spatial_conv(row_padded, w_spatial):
    out = lax.conv_general_dilated(
        row_padded,
        w_spatial,
        window_strides=(1, 1),
        padding=((0, 0), (1, 1)),
        dimension_numbers=("NHWC", "HWIO", "NHWC"),
        preferred_element_type=jnp.float32,
    )
    return out.astype(jnp.bfloat16)


def group_stats(conv_out, weight):
    cout_width = conv_out.shape[-1]
    per_group = cout_width // GROUPS
    values = conv_out.astype(jnp.float32).reshape(-1, cout_width)
    sums = jnp.sum(values, axis=0).reshape(GROUPS, per_group).sum(axis=1) * weight
    squares = jnp.sum(values * values, axis=0).reshape(GROUPS, per_group).sum(axis=1) * weight
    return sums, squares


def normalize(conv_out, sums, squares, cell_count, norm_gain, norm_shift):
    per_group = conv_out.shape[-1] // GROUPS
    group_mean = sums / cell_count
    group_var = squares / cell_count - group_mean * group_mean
    inv_scale = lax.rsqrt(group_var + 1e-06)
    mean_chan = jnp.repeat(group_mean, per_group)
    scale_chan = jnp.repeat(inv_scale, per_group)
    values = conv_out.astype(jnp.float32)
    return jax.nn.silu((values - mean_chan) * scale_chan * norm_gain + norm_shift).astype(
        jnp.bfloat16
    )


def time_conv(activated, w_time, time_bias, out_frames):
    first = activated[0:1]
    even = activated[0::2][:out_frames]
    odd = activated[1::2][: out_frames - 1]
    taps = [
        jnp.concatenate([first, even[: out_frames - 1]], axis=0),
        jnp.concatenate([first, odd], axis=0),
        even,
    ]
    stacked = jnp.concatenate(taps, axis=-1)
    weights = w_time.reshape(-1, w_time.shape[-1])
    product = jnp.einsum("trwc,cd->trwd", stacked, weights, preferred_element_type=jnp.float32)
    return (product + time_bias).astype(jnp.bfloat16)


def encode_stats(stats):
    high = stats.astype(jnp.bfloat16)
    low = (stats - high.astype(jnp.float32)).astype(jnp.bfloat16)
    return jnp.concatenate([high, low])


def decode_stats(coded, width):
    values = coded.astype(jnp.float32)
    return jnp.sum(values[:, :width], axis=0) + jnp.sum(values[:, width : 2 * width], axis=0)


def shards(clip_frames, frame_of_slot, w_spatial, norm_gain, norm_shift, w_time, time_bias):
    tm_count = lax.axis_size("tm")
    height_count = lax.axis_size("height")
    live_frames = tm_count // 2 + 1
    out_frames = (live_frames - 1) // 2 + 1
    frame_slots = slot_lookup(frame_of_slot, live_frames)
    padded = with_halo(clip_frames, (("height", 1),), 1)
    staged, chan_sums, chan_squares = conv_call(padded[0], w_spatial)
    cols = padded.shape[2]
    tail = staged.shape[1] - 1
    own_frame = lax.dynamic_index_in_dim(frame_of_slot, lax.axis_index("tm"), 0, keepdims=False)
    weight = jnp.where(own_frame >= 0, 1.0, 0.0).astype(jnp.float32)
    per_group = w_spatial.shape[-1] // GROUPS
    sums = chan_sums.reshape(GROUPS, per_group).sum(axis=1) * weight
    squares = chan_squares.reshape(GROUPS, per_group).sum(axis=1) * weight
    coded = encode_stats(jnp.concatenate([sums, squares]))
    column = jnp.zeros((staged.shape[-1],), jnp.bfloat16).at[: coded.shape[0]].set(coded)
    payload = staged.at[:, tail, :].set(jnp.broadcast_to(column, (staged.shape[0], column.shape[0])))
    received = lax.all_to_all(payload[None], "tm", split_axis=1, concat_axis=0, tiled=True)
    partial = decode_stats(received[:, 0, tail, : coded.shape[0]], 2 * GROUPS)
    other = lax.ppermute(partial, "height", [(0, 1), (1, 0)])
    totals = partial + other
    sums, squares = totals[:GROUPS], totals[GROUPS:]
    cell_count = float(live_frames * clip_frames.shape[1] * height_count * cols * per_group)
    group_mean = sums / cell_count
    group_var = squares / cell_count - group_mean * group_mean
    inv_scale = lax.rsqrt(group_var + 1e-06)
    latent = latent_call(
        frame_slots.astype(jnp.int32),
        received.reshape(received.shape[0], tail + 1, -1),
        w_time,
        jnp.repeat(group_mean, per_group),
        jnp.repeat(inv_scale, per_group),
        norm_gain,
        norm_shift,
        time_bias,
        out_frames,
        cols,
    )
    latent = latent.reshape(out_frames, 1, cols, latent.shape[-1])
    return latent.reshape(out_frames, 1, latent.shape[1], latent.shape[2], latent.shape[3])


def solution(mesh):
    return jax.shard_map(
        shards,
        mesh=mesh,
        in_specs=(P(("dp", "tm"), "height", None, None), P("dp"), P(), P(), P(), P(), P()),
        out_specs=P("dp", "height", "tm", None, None),
        check_vma=False,
    )
```

```python
import functools

import jax
import jax.numpy as jnp
import numpy as np
from jax import lax
from jax.experimental import pallas as pl
from jax.experimental.pallas import tpu as pltpu
from jax.sharding import PartitionSpec as P

GROUPS = 32


def with_halo(block, sides, width):
    for axis, dim in sides:
        count = lax.axis_size(axis)
        forward = [(i, i + 1) for i in range(count - 1)]
        backward = [(target, source) for source, target in forward]
        low = lax.ppermute(
            lax.slice_in_dim(block, block.shape[dim] - width, None, axis=dim), axis, forward
        )
        high = lax.ppermute(lax.slice_in_dim(block, 0, width, axis=dim), axis, backward)
        block = jnp.concatenate([low, block, high], axis=dim)
    return block


def slot_lookup(frame_of_slot, live_frames):
    wanted = jnp.arange(live_frames, dtype=jnp.int32)[:, None]
    places = jnp.arange(frame_of_slot.shape[0], dtype=jnp.int32)[None, :]
    matches = frame_of_slot[None, :] == wanted
    return jnp.sum(jnp.where(matches, places, 0), axis=1)


def conv_kernel(low_ref, high_ref, block_ref, w_ref, out_ref, sum_ref, sq_ref, x_ref, sem, *, chunk, cols):
    step = pl.program_id(0)
    rows = block_ref.shape[0]

    @pl.when(step == 0)
    def _():
        fetch = pltpu.make_async_copy(block_ref, x_ref.at[pl.ds(1, rows)], sem)
        fetch.start()
        x_ref[0:1] = low_ref[...]
        x_ref[rows + 1 : rows + 2] = high_ref[...]
        fetch.wait()

    base = step * chunk
    m = chunk * cols
    parts = []
    for col_tap in range(3):
        acc = None
        for row_tap in range(3):
            xs = x_ref[pl.ds(base + row_tap, chunk), :, :].reshape(m, x_ref.shape[-1])
            p = jnp.dot(xs, w_ref[row_tap, col_tap], preferred_element_type=jnp.float32)
            acc = p if acc is None else acc + p
        parts.append(acc)
    col = lax.broadcasted_iota(jnp.int32, (m, 1), 0) % cols
    left = jnp.where(col == 0, 0.0, pltpu.roll(parts[0], 1, 0))
    right = jnp.where(col == cols - 1, 0.0, pltpu.roll(parts[2], m - 1, 0))
    total = (left + parts[1]) + right
    rounded = total.astype(jnp.bfloat16)
    lanes = out_ref.shape[-1]
    for quarter in range(rounded.shape[-1] // lanes):
        piece = rounded[:, quarter * lanes : (quarter + 1) * lanes]
        out_ref[:, quarter * cols : (quarter + 1) * cols, :] = piece.reshape(chunk, cols, lanes)
    tail = out_ref.shape[1] - 1
    out_ref[:, tail : tail + 1, :] = jnp.zeros((chunk, 1, lanes), jnp.bfloat16)
    values = rounded.astype(jnp.float32)

    @pl.when(step == 0)
    def _():
        sum_ref[...] = jnp.zeros_like(sum_ref)
        sq_ref[...] = jnp.zeros_like(sq_ref)

    sum_ref[...] += jnp.sum(values, axis=0, keepdims=True)
    sq_ref[...] += jnp.sum(values * values, axis=0, keepdims=True)

def conv_call(low, high, block, w, chunk=8, lanes=128):
    rows, cols, cin = block.shape
    cout = w.shape[-1]
    stacked = cols * (cout // lanes) + 1
    halo = pl.BlockSpec((1, cols, cin), lambda i: (0, 0, 0))
    return pl.pallas_call(
        functools.partial(conv_kernel, chunk=chunk, cols=cols),
        grid=(rows // chunk,),
        in_specs=[
            halo,
            halo,
            pl.BlockSpec(memory_space=pl.ANY),
            pl.BlockSpec((3, 3, cin, cout), lambda i: (0, 0, 0, 0)),
        ],
        out_specs=[
            pl.BlockSpec((chunk, stacked, lanes), lambda i: (i, 0, 0)),
            pl.BlockSpec((1, cout), lambda i: (0, 0)),
            pl.BlockSpec((1, cout), lambda i: (0, 0)),
        ],
        out_shape=[
            jax.ShapeDtypeStruct((rows, stacked, lanes), jnp.bfloat16),
            jax.ShapeDtypeStruct((1, cout), jnp.float32),
            jax.ShapeDtypeStruct((1, cout), jnp.float32),
        ],
        scratch_shapes=[pltpu.VMEM((rows + 2, cols, cin), block.dtype), pltpu.SemaphoreType.DMA(())],
        compiler_params=pltpu.CompilerParams(dimension_semantics=("arbitrary",)),
    )(low, high, block, w)

def latent_kernel(slots_ref, x_ref, w_ref, mean_ref, scale_ref, gain_ref, shift_ref, bias_ref, out_ref, tap0_ref, tap1_ref, tap2_ref):
    live = 2 * out_ref.shape[0] - 1
    cols, chans = out_ref.shape[1], out_ref.shape[2]
    for frame in range(live):
        slot = slots_ref[frame]
        lanes = x_ref.shape[-1]
        pieces = [x_ref[slot, pl.ds(q * cols, cols), :] for q in range(chans // lanes)]
        values = jnp.concatenate(pieces, axis=-1).astype(jnp.float32)
        normed = (values - mean_ref[...]) * scale_ref[...] * gain_ref[...] + shift_ref[...]
        activated = jax.nn.silu(normed).astype(jnp.bfloat16)
        if frame == 0:
            tap0_ref[0] = activated
            tap1_ref[0] = activated
        if frame % 2 == 0:
            tap2_ref[frame // 2] = activated
            if frame // 2 + 1 < out_ref.shape[0]:
                tap0_ref[frame // 2 + 1] = activated
        else:
            tap1_ref[(frame + 1) // 2] = activated
    rows = out_ref.shape[0] * cols
    running = bias_ref[...]
    for time_tap, tap_ref in enumerate((tap0_ref, tap1_ref, tap2_ref)):
        block = tap_ref[...].reshape(rows, chans)
        running = running + jnp.dot(block, w_ref[time_tap], preferred_element_type=jnp.float32)
    out_ref[...] = running.astype(jnp.bfloat16).reshape(out_ref.shape)


def latent_call(frame_slots, received, w_time, mean_chan, scale_chan, norm_gain, norm_shift, time_bias, out_frames, cols):
    chans = w_time.shape[-1]
    vmem = pltpu.MemorySpace.VMEM if hasattr(pltpu, "MemorySpace") else pltpu.TPUMemorySpace.VMEM
    smem = pltpu.MemorySpace.SMEM if hasattr(pltpu, "MemorySpace") else pltpu.TPUMemorySpace.SMEM
    row = lambda v: v.reshape(1, chans).astype(jnp.float32)
    tap = pltpu.VMEM((out_frames, cols, chans), jnp.bfloat16)
    return pl.pallas_call(
        latent_kernel,
        in_specs=[pl.BlockSpec(memory_space=smem)] + [pl.BlockSpec(memory_space=vmem)] * 7,
        out_specs=pl.BlockSpec(memory_space=vmem),
        out_shape=jax.ShapeDtypeStruct((out_frames, cols, chans), jnp.bfloat16),
        scratch_shapes=[tap, tap, tap],
    )(
        frame_slots, received, w_time,
        row(mean_chan), row(scale_chan), row(norm_gain), row(norm_shift), row(time_bias),
    )

def spatial_conv(row_padded, w_spatial):
    out = lax.conv_general_dilated(
        row_padded,
        w_spatial,
        window_strides=(1, 1),
        padding=((0, 0), (1, 1)),
        dimension_numbers=("NHWC", "HWIO", "NHWC"),
        preferred_element_type=jnp.float32,
    )
    return out.astype(jnp.bfloat16)


def group_stats(conv_out, weight):
    cout_width = conv_out.shape[-1]
    per_group = cout_width // GROUPS
    values = conv_out.astype(jnp.float32).reshape(-1, cout_width)
    sums = jnp.sum(values, axis=0).reshape(GROUPS, per_group).sum(axis=1) * weight
    squares = jnp.sum(values * values, axis=0).reshape(GROUPS, per_group).sum(axis=1) * weight
    return sums, squares


def normalize(conv_out, sums, squares, cell_count, norm_gain, norm_shift):
    per_group = conv_out.shape[-1] // GROUPS
    group_mean = sums / cell_count
    group_var = squares / cell_count - group_mean * group_mean
    inv_scale = lax.rsqrt(group_var + 1e-06)
    mean_chan = jnp.repeat(group_mean, per_group)
    scale_chan = jnp.repeat(inv_scale, per_group)
    values = conv_out.astype(jnp.float32)
    return jax.nn.silu((values - mean_chan) * scale_chan * norm_gain + norm_shift).astype(
        jnp.bfloat16
    )


def time_conv(activated, w_time, time_bias, out_frames):
    first = activated[0:1]
    even = activated[0::2][:out_frames]
    odd = activated[1::2][: out_frames - 1]
    taps = [
        jnp.concatenate([first, even[: out_frames - 1]], axis=0),
        jnp.concatenate([first, odd], axis=0),
        even,
    ]
    stacked = jnp.concatenate(taps, axis=-1)
    weights = w_time.reshape(-1, w_time.shape[-1])
    product = jnp.einsum("trwc,cd->trwd", stacked, weights, preferred_element_type=jnp.float32)
    return (product + time_bias).astype(jnp.bfloat16)


def encode_stats(stats):
    high = stats.astype(jnp.bfloat16)
    low = (stats - high.astype(jnp.float32)).astype(jnp.bfloat16)
    return jnp.concatenate([high, low])


def decode_stats(coded, width):
    values = coded.astype(jnp.float32)
    return jnp.sum(values[:, :width], axis=0) + jnp.sum(values[:, width : 2 * width], axis=0)


def shards(clip_frames, frame_of_slot, w_spatial, norm_gain, norm_shift, w_time, time_bias):
    tm_count = lax.axis_size("tm")
    height_count = lax.axis_size("height")
    live_frames = tm_count // 2 + 1
    out_frames = (live_frames - 1) // 2 + 1
    frame_slots = slot_lookup(frame_of_slot, live_frames)
    count = lax.axis_size("height")
    forward = [(i, i + 1) for i in range(count - 1)]
    backward = [(target, source) for source, target in forward]
    low = lax.ppermute(clip_frames[0, -1:], "height", forward)
    high = lax.ppermute(clip_frames[0, :1], "height", backward)
    staged, chan_sums, chan_squares = conv_call(low, high, clip_frames[0], w_spatial)
    cols = clip_frames.shape[2]
    tail = staged.shape[1] - 1
    own_frame = lax.dynamic_index_in_dim(frame_of_slot, lax.axis_index("tm"), 0, keepdims=False)
    weight = jnp.where(own_frame >= 0, 1.0, 0.0).astype(jnp.float32)
    per_group = w_spatial.shape[-1] // GROUPS
    sums = chan_sums.reshape(GROUPS, per_group).sum(axis=1) * weight
    squares = chan_squares.reshape(GROUPS, per_group).sum(axis=1) * weight
    coded = encode_stats(jnp.concatenate([sums, squares]))
    column = jnp.zeros((staged.shape[-1],), jnp.bfloat16).at[: coded.shape[0]].set(coded)
    payload = staged.at[:, tail, :].set(jnp.broadcast_to(column, (staged.shape[0], column.shape[0])))
    received = lax.all_to_all(payload[None], "tm", split_axis=1, concat_axis=0, tiled=True)
    partial = decode_stats(received[:, 0, tail, : coded.shape[0]], 2 * GROUPS)
    other = lax.ppermute(partial, "height", [(0, 1), (1, 0)])
    totals = partial + other
    sums, squares = totals[:GROUPS], totals[GROUPS:]
    cell_count = float(live_frames * clip_frames.shape[1] * height_count * cols * per_group)
    group_mean = sums / cell_count
    group_var = squares / cell_count - group_mean * group_mean
    inv_scale = lax.rsqrt(group_var + 1e-06)
    latent = latent_call(
        frame_slots.astype(jnp.int32),
        received.reshape(received.shape[0], tail + 1, -1),
        w_time,
        jnp.repeat(group_mean, per_group),
        jnp.repeat(inv_scale, per_group),
        norm_gain,
        norm_shift,
        time_bias,
        out_frames,
        cols,
    )
    latent = latent.reshape(out_frames, 1, cols, latent.shape[-1])
    return latent.reshape(out_frames, 1, latent.shape[1], latent.shape[2], latent.shape[3])


def solution(mesh):
    return jax.shard_map(
        shards,
        mesh=mesh,
        in_specs=(P(("dp", "tm"), "height", None, None), P("dp"), P(), P(), P(), P(), P()),
        out_specs=P("dp", "height", "tm", None, None),
        check_vma=False,
    )
```

```python
import functools

import jax
import jax.numpy as jnp
import numpy as np
from jax import lax
from jax.experimental import pallas as pl
from jax.experimental.pallas import tpu as pltpu
from jax.sharding import PartitionSpec as P

GROUPS = 32


def with_halo(block, sides, width):
    for axis, dim in sides:
        count = lax.axis_size(axis)
        forward = [(i, i + 1) for i in range(count - 1)]
        backward = [(target, source) for source, target in forward]
        low = lax.ppermute(
            lax.slice_in_dim(block, block.shape[dim] - width, None, axis=dim), axis, forward
        )
        high = lax.ppermute(lax.slice_in_dim(block, 0, width, axis=dim), axis, backward)
        block = jnp.concatenate([low, block, high], axis=dim)
    return block


def slot_lookup(frame_of_slot, live_frames):
    wanted = jnp.arange(live_frames, dtype=jnp.int32)[:, None]
    places = jnp.arange(frame_of_slot.shape[0], dtype=jnp.int32)[None, :]
    matches = frame_of_slot[None, :] == wanted
    return jnp.sum(jnp.where(matches, places, 0), axis=1)


def conv_kernel(fos_ref, low_ref, high_ref, block_ref, w_ref, out_ref, sum_ref, sq_ref, code_ref, x_ref, sem, *, chunk, cols, groups):
    step = pl.program_id(0)
    rows = block_ref.shape[0]

    @pl.when(step == 0)
    def _():
        fetch = pltpu.make_async_copy(block_ref, x_ref.at[pl.ds(1, rows)], sem)
        fetch.start()
        x_ref[0:1] = low_ref[...]
        x_ref[rows + 1 : rows + 2] = high_ref[...]
        fetch.wait()

    base = step * chunk
    m = chunk * cols
    parts = []
    for col_tap in range(3):
        acc = None
        for row_tap in range(3):
            xs = x_ref[pl.ds(base + row_tap, chunk), :, :].reshape(m, x_ref.shape[-1])
            p = jnp.dot(xs, w_ref[row_tap, col_tap], preferred_element_type=jnp.float32)
            acc = p if acc is None else acc + p
        parts.append(acc)
    col = lax.broadcasted_iota(jnp.int32, (m, 1), 0) % cols
    left = jnp.where(col == 0, 0.0, pltpu.roll(parts[0], 1, 0))
    right = jnp.where(col == cols - 1, 0.0, pltpu.roll(parts[2], m - 1, 0))
    total = (left + parts[1]) + right
    rounded = total.astype(jnp.bfloat16)
    lanes = out_ref.shape[-1]
    for quarter in range(rounded.shape[-1] // lanes):
        piece = rounded[:, quarter * lanes : (quarter + 1) * lanes]
        out_ref[:, quarter * cols : (quarter + 1) * cols, :] = piece.reshape(chunk, cols, lanes)
    tail = out_ref.shape[1] - 1
    out_ref[:, tail : tail + 1, :] = jnp.zeros((chunk, 1, lanes), jnp.bfloat16)
    values = rounded.astype(jnp.float32)

    @pl.when(step == 0)
    def _():
        sum_ref[...] = jnp.zeros_like(sum_ref)
        sq_ref[...] = jnp.zeros_like(sq_ref)

    sum_ref[...] += jnp.sum(values, axis=0, keepdims=True)
    sq_ref[...] += jnp.sum(values * values, axis=0, keepdims=True)

    @pl.when(step == pl.num_programs(0) - 1)
    def _():
        chans = sum_ref.shape[-1]
        width = code_ref.shape[-1]
        per_group = chans // groups
        chan = lax.broadcasted_iota(jnp.int32, (chans, width), 0) // per_group
        lane = lax.broadcasted_iota(jnp.int32, (chans, width), 1)
        to_sums = jnp.where(chan == lane, 1.0, 0.0)
        to_squares = jnp.where(chan + groups == lane, 1.0, 0.0)
        exact = lax.Precision.HIGHEST
        grouped = jnp.dot(sum_ref[...], to_sums, precision=exact, preferred_element_type=jnp.float32)
        grouped = grouped + jnp.dot(sq_ref[...], to_squares, precision=exact, preferred_element_type=jnp.float32)
        own = fos_ref[lax.axis_index("tm")]
        grouped = grouped * jnp.where(own >= 0, 1.0, 0.0)
        high = grouped.astype(jnp.bfloat16).astype(jnp.float32)
        low = pltpu.roll(grouped - high, 2 * groups, 1)
        out_lane = lax.broadcasted_iota(jnp.int32, (1, width), 1)
        code_ref[...] = jnp.where(out_lane < 2 * groups, high, low).astype(jnp.bfloat16)

def conv_call(frame_of_slot, low, high, block, w, chunk=8, lanes=128):
    rows, cols, cin = block.shape
    cout = w.shape[-1]
    stacked = cols * (cout // lanes) + 1
    halo = pl.BlockSpec((1, cols, cin), lambda i: (0, 0, 0))
    return pl.pallas_call(
        functools.partial(conv_kernel, chunk=chunk, cols=cols, groups=GROUPS),
        grid=(rows // chunk,),
        in_specs=[
            pl.BlockSpec(memory_space=pltpu.SMEM),
            halo,
            halo,
            pl.BlockSpec(memory_space=pl.ANY),
            pl.BlockSpec((3, 3, cin, cout), lambda i: (0, 0, 0, 0)),
        ],
        out_specs=[
            pl.BlockSpec((chunk, stacked, lanes), lambda i: (i, 0, 0)),
            pl.BlockSpec((1, cout), lambda i: (0, 0)),
            pl.BlockSpec((1, cout), lambda i: (0, 0)),
            pl.BlockSpec((1, lanes), lambda i: (0, 0)),
        ],
        out_shape=[
            jax.ShapeDtypeStruct((rows, stacked, lanes), jnp.bfloat16),
            jax.ShapeDtypeStruct((1, cout), jnp.float32),
            jax.ShapeDtypeStruct((1, cout), jnp.float32),
            jax.ShapeDtypeStruct((1, lanes), jnp.bfloat16),
        ],
        scratch_shapes=[pltpu.VMEM((rows + 2, cols, cin), block.dtype), pltpu.SemaphoreType.DMA(())],
        compiler_params=pltpu.CompilerParams(dimension_semantics=("arbitrary",)),
    )(frame_of_slot, low, high, block, w)

def latent_kernel(slots_ref, x_ref, w_ref, mean_ref, scale_ref, gain_ref, shift_ref, bias_ref, out_ref, tap0_ref, tap1_ref, tap2_ref):
    live = 2 * out_ref.shape[0] - 1
    cols, chans = out_ref.shape[1], out_ref.shape[2]
    for frame in range(live):
        slot = slots_ref[frame]
        lanes = x_ref.shape[-1]
        pieces = [x_ref[slot, pl.ds(q * cols, cols), :] for q in range(chans // lanes)]
        values = jnp.concatenate(pieces, axis=-1).astype(jnp.float32)
        normed = (values - mean_ref[...]) * scale_ref[...] * gain_ref[...] + shift_ref[...]
        activated = jax.nn.silu(normed).astype(jnp.bfloat16)
        if frame == 0:
            tap0_ref[0] = activated
            tap1_ref[0] = activated
        if frame % 2 == 0:
            tap2_ref[frame // 2] = activated
            if frame // 2 + 1 < out_ref.shape[0]:
                tap0_ref[frame // 2 + 1] = activated
        else:
            tap1_ref[(frame + 1) // 2] = activated
    rows = out_ref.shape[0] * cols
    running = bias_ref[...]
    for time_tap, tap_ref in enumerate((tap0_ref, tap1_ref, tap2_ref)):
        block = tap_ref[...].reshape(rows, chans)
        running = running + jnp.dot(block, w_ref[time_tap], preferred_element_type=jnp.float32)
    out_ref[...] = running.astype(jnp.bfloat16).reshape(out_ref.shape)


def latent_call(frame_slots, received, w_time, mean_chan, scale_chan, norm_gain, norm_shift, time_bias, out_frames, cols):
    chans = w_time.shape[-1]
    vmem = pltpu.MemorySpace.VMEM if hasattr(pltpu, "MemorySpace") else pltpu.TPUMemorySpace.VMEM
    smem = pltpu.MemorySpace.SMEM if hasattr(pltpu, "MemorySpace") else pltpu.TPUMemorySpace.SMEM
    row = lambda v: v.reshape(1, chans).astype(jnp.float32)
    tap = pltpu.VMEM((out_frames, cols, chans), jnp.bfloat16)
    return pl.pallas_call(
        latent_kernel,
        in_specs=[pl.BlockSpec(memory_space=smem)] + [pl.BlockSpec(memory_space=vmem)] * 7,
        out_specs=pl.BlockSpec(memory_space=vmem),
        out_shape=jax.ShapeDtypeStruct((out_frames, cols, chans), jnp.bfloat16),
        scratch_shapes=[tap, tap, tap],
    )(
        frame_slots, received, w_time,
        row(mean_chan), row(scale_chan), row(norm_gain), row(norm_shift), row(time_bias),
    )

def spatial_conv(row_padded, w_spatial):
    out = lax.conv_general_dilated(
        row_padded,
        w_spatial,
        window_strides=(1, 1),
        padding=((0, 0), (1, 1)),
        dimension_numbers=("NHWC", "HWIO", "NHWC"),
        preferred_element_type=jnp.float32,
    )
    return out.astype(jnp.bfloat16)


def group_stats(conv_out, weight):
    cout_width = conv_out.shape[-1]
    per_group = cout_width // GROUPS
    values = conv_out.astype(jnp.float32).reshape(-1, cout_width)
    sums = jnp.sum(values, axis=0).reshape(GROUPS, per_group).sum(axis=1) * weight
    squares = jnp.sum(values * values, axis=0).reshape(GROUPS, per_group).sum(axis=1) * weight
    return sums, squares


def normalize(conv_out, sums, squares, cell_count, norm_gain, norm_shift):
    per_group = conv_out.shape[-1] // GROUPS
    group_mean = sums / cell_count
    group_var = squares / cell_count - group_mean * group_mean
    inv_scale = lax.rsqrt(group_var + 1e-06)
    mean_chan = jnp.repeat(group_mean, per_group)
    scale_chan = jnp.repeat(inv_scale, per_group)
    values = conv_out.astype(jnp.float32)
    return jax.nn.silu((values - mean_chan) * scale_chan * norm_gain + norm_shift).astype(
        jnp.bfloat16
    )


def time_conv(activated, w_time, time_bias, out_frames):
    first = activated[0:1]
    even = activated[0::2][:out_frames]
    odd = activated[1::2][: out_frames - 1]
    taps = [
        jnp.concatenate([first, even[: out_frames - 1]], axis=0),
        jnp.concatenate([first, odd], axis=0),
        even,
    ]
    stacked = jnp.concatenate(taps, axis=-1)
    weights = w_time.reshape(-1, w_time.shape[-1])
    product = jnp.einsum("trwc,cd->trwd", stacked, weights, preferred_element_type=jnp.float32)
    return (product + time_bias).astype(jnp.bfloat16)


def encode_stats(stats):
    high = stats.astype(jnp.bfloat16)
    low = (stats - high.astype(jnp.float32)).astype(jnp.bfloat16)
    return jnp.concatenate([high, low])


def decode_stats(coded, width):
    values = coded.astype(jnp.float32)
    return jnp.sum(values[:, :width], axis=0) + jnp.sum(values[:, width : 2 * width], axis=0)


def shards(clip_frames, frame_of_slot, w_spatial, norm_gain, norm_shift, w_time, time_bias):
    tm_count = lax.axis_size("tm")
    height_count = lax.axis_size("height")
    live_frames = tm_count // 2 + 1
    out_frames = (live_frames - 1) // 2 + 1
    frame_slots = slot_lookup(frame_of_slot, live_frames)
    count = lax.axis_size("height")
    forward = [(i, i + 1) for i in range(count - 1)]
    backward = [(target, source) for source, target in forward]
    low = lax.ppermute(clip_frames[0, -1:], "height", forward)
    high = lax.ppermute(clip_frames[0, :1], "height", backward)
    staged, _, _, coded = conv_call(frame_of_slot, low, high, clip_frames[0], w_spatial)
    cols = clip_frames.shape[2]
    tail = staged.shape[1] - 1
    per_group = w_spatial.shape[-1] // GROUPS
    column = coded[0]
    payload = staged.at[:, tail, :].set(jnp.broadcast_to(column, (staged.shape[0], column.shape[0])))
    received = lax.all_to_all(payload[None], "tm", split_axis=1, concat_axis=0, tiled=True)
    partial = decode_stats(received[:, 0, tail, :], 2 * GROUPS)
    other = lax.ppermute(partial, "height", [(0, 1), (1, 0)])
    totals = partial + other
    sums, squares = totals[:GROUPS], totals[GROUPS:]
    cell_count = float(live_frames * clip_frames.shape[1] * height_count * cols * per_group)
    group_mean = sums / cell_count
    group_var = squares / cell_count - group_mean * group_mean
    inv_scale = lax.rsqrt(group_var + 1e-06)
    latent = latent_call(
        frame_slots.astype(jnp.int32),
        received.reshape(received.shape[0], tail + 1, -1),
        w_time,
        jnp.repeat(group_mean, per_group),
        jnp.repeat(inv_scale, per_group),
        norm_gain,
        norm_shift,
        time_bias,
        out_frames,
        cols,
    )
    latent = latent.reshape(out_frames, 1, cols, latent.shape[-1])
    return latent.reshape(out_frames, 1, latent.shape[1], latent.shape[2], latent.shape[3])


def solution(mesh):
    return jax.shard_map(
        shards,
        mesh=mesh,
        in_specs=(P(("dp", "tm"), "height", None, None), P("dp"), P(), P(), P(), P(), P()),
        out_specs=P("dp", "height", "tm", None, None),
        check_vma=False,
    )
```

```python
import functools

import jax
import jax.numpy as jnp
import numpy as np
from jax import lax
from jax.experimental import pallas as pl
from jax.experimental.pallas import tpu as pltpu
from jax.sharding import PartitionSpec as P

GROUPS = 32


def with_halo(block, sides, width):
    for axis, dim in sides:
        count = lax.axis_size(axis)
        forward = [(i, i + 1) for i in range(count - 1)]
        backward = [(target, source) for source, target in forward]
        low = lax.ppermute(
            lax.slice_in_dim(block, block.shape[dim] - width, None, axis=dim), axis, forward
        )
        high = lax.ppermute(lax.slice_in_dim(block, 0, width, axis=dim), axis, backward)
        block = jnp.concatenate([low, block, high], axis=dim)
    return block


def slot_lookup(frame_of_slot, live_frames):
    wanted = jnp.arange(live_frames, dtype=jnp.int32)[:, None]
    places = jnp.arange(frame_of_slot.shape[0], dtype=jnp.int32)[None, :]
    matches = frame_of_slot[None, :] == wanted
    return jnp.sum(jnp.where(matches, places, 0), axis=1)


def conv_kernel(fos_ref, low_ref, high_ref, block_ref, w_ref, out_ref, sum_ref, sq_ref, code_ref, x_ref, sem, *, chunk, cols, groups):
    step = pl.program_id(0)
    rows = block_ref.shape[0]

    @pl.when(step == 0)
    def _():
        fetch = pltpu.make_async_copy(block_ref, x_ref.at[pl.ds(1, rows)], sem)
        fetch.start()
        x_ref[0:1] = low_ref[...]
        x_ref[rows + 1 : rows + 2] = high_ref[...]
        fetch.wait()

    base = step * chunk
    m = chunk * cols
    parts = []
    for col_tap in range(3):
        acc = None
        for row_tap in range(3):
            xs = x_ref[pl.ds(base + row_tap, chunk), :, :].reshape(m, x_ref.shape[-1])
            p = jnp.dot(xs, w_ref[row_tap, col_tap], preferred_element_type=jnp.float32)
            acc = p if acc is None else acc + p
        parts.append(acc)
    col = lax.broadcasted_iota(jnp.int32, (m, 1), 0) % cols
    left = jnp.where(col == 0, 0.0, pltpu.roll(parts[0], 1, 0))
    right = jnp.where(col == cols - 1, 0.0, pltpu.roll(parts[2], m - 1, 0))
    total = (left + parts[1]) + right
    rounded = total.astype(jnp.bfloat16)
    lanes = out_ref.shape[-1]
    for quarter in range(rounded.shape[-1] // lanes):
        piece = rounded[:, quarter * lanes : (quarter + 1) * lanes]
        out_ref[:, quarter * cols : (quarter + 1) * cols, :] = piece.reshape(chunk, cols, lanes)
    tail = out_ref.shape[1] - 1
    out_ref[:, tail : tail + 1, :] = jnp.zeros((chunk, 1, lanes), jnp.bfloat16)
    values = rounded.astype(jnp.float32)

    @pl.when(step == 0)
    def _():
        sum_ref[...] = jnp.zeros_like(sum_ref)
        sq_ref[...] = jnp.zeros_like(sq_ref)

    sum_ref[...] += jnp.sum(values, axis=0, keepdims=True)
    sq_ref[...] += jnp.sum(values * values, axis=0, keepdims=True)

    @pl.when(step == pl.num_programs(0) - 1)
    def _():
        chans = sum_ref.shape[-1]
        width = code_ref.shape[-1]
        per_group = chans // groups
        chan = lax.broadcasted_iota(jnp.int32, (chans, width), 0) // per_group
        lane = lax.broadcasted_iota(jnp.int32, (chans, width), 1)
        to_sums = jnp.where(chan == lane, 1.0, 0.0)
        to_squares = jnp.where(chan + groups == lane, 1.0, 0.0)
        exact = lax.Precision.HIGHEST
        grouped = jnp.dot(sum_ref[...], to_sums, precision=exact, preferred_element_type=jnp.float32)
        grouped = grouped + jnp.dot(sq_ref[...], to_squares, precision=exact, preferred_element_type=jnp.float32)
        own = fos_ref[lax.axis_index("tm")]
        grouped = grouped * jnp.where(own >= 0, 1.0, 0.0)
        high = grouped.astype(jnp.bfloat16).astype(jnp.float32)
        low = pltpu.roll(grouped - high, 2 * groups, 1)
        out_lane = lax.broadcasted_iota(jnp.int32, (1, width), 1)
        code_ref[...] = jnp.where(out_lane < 2 * groups, high, low).astype(jnp.bfloat16)

def conv_call(frame_of_slot, low, high, block, w, chunk=8, lanes=128):
    rows, cols, cin = block.shape
    cout = w.shape[-1]
    stacked = cols * (cout // lanes) + 1
    halo = pl.BlockSpec((1, cols, cin), lambda i: (0, 0, 0))
    return pl.pallas_call(
        functools.partial(conv_kernel, chunk=chunk, cols=cols, groups=GROUPS),
        grid=(rows // chunk,),
        in_specs=[
            pl.BlockSpec(memory_space=pltpu.SMEM),
            halo,
            halo,
            pl.BlockSpec(memory_space=pl.ANY),
            pl.BlockSpec((3, 3, cin, cout), lambda i: (0, 0, 0, 0)),
        ],
        out_specs=[
            pl.BlockSpec((chunk, stacked, lanes), lambda i: (i, 0, 0)),
            pl.BlockSpec((1, cout), lambda i: (0, 0)),
            pl.BlockSpec((1, cout), lambda i: (0, 0)),
            pl.BlockSpec((1, lanes), lambda i: (0, 0)),
        ],
        out_shape=[
            jax.ShapeDtypeStruct((rows, stacked, lanes), jnp.bfloat16),
            jax.ShapeDtypeStruct((1, cout), jnp.float32),
            jax.ShapeDtypeStruct((1, cout), jnp.float32),
            jax.ShapeDtypeStruct((1, lanes), jnp.bfloat16),
        ],
        scratch_shapes=[pltpu.VMEM((rows + 2, cols, cin), block.dtype), pltpu.SemaphoreType.DMA(())],
        compiler_params=pltpu.CompilerParams(dimension_semantics=("arbitrary",)),
    )(frame_of_slot, low, high, block, w)

def latent_kernel(slots_ref, x_ref, w_ref, totals_ref, gain_ref, shift_ref, bias_ref, out_ref, tap0_ref, tap1_ref, tap2_ref, *, cell_count, groups):
    live = 2 * out_ref.shape[0] - 1
    cols, chans = out_ref.shape[1], out_ref.shape[2]
    width = totals_ref.shape[-1]
    totals = totals_ref[...]
    lane = lax.broadcasted_iota(jnp.int32, (1, width), 1)
    group_mean = totals / cell_count
    group_var = pltpu.roll(totals, width - groups, 1) / cell_count - group_mean * group_mean
    inv_scale = lax.rsqrt(group_var + 1e-06)
    group_mean = jnp.where(lane < groups, group_mean, 0.0)
    inv_scale = jnp.where(lane < groups, inv_scale, 0.0)
    owner = lax.broadcasted_iota(jnp.int32, (width, chans), 1) // (chans // groups)
    expand = jnp.where(owner == lax.broadcasted_iota(jnp.int32, (width, chans), 0), 1.0, 0.0)
    exact = lax.Precision.HIGHEST
    mean_chan = jnp.dot(group_mean, expand, precision=exact, preferred_element_type=jnp.float32)
    scale_chan = jnp.dot(inv_scale, expand, precision=exact, preferred_element_type=jnp.float32)
    for frame in range(live):
        slot = slots_ref[frame]
        lanes = x_ref.shape[-1]
        pieces = [x_ref[slot, pl.ds(q * cols, cols), :] for q in range(chans // lanes)]
        values = jnp.concatenate(pieces, axis=-1).astype(jnp.float32)
        normed = (values - mean_chan) * scale_chan * gain_ref[...] + shift_ref[...]
        activated = jax.nn.silu(normed).astype(jnp.bfloat16)
        if frame == 0:
            tap0_ref[0] = activated
            tap1_ref[0] = activated
        if frame % 2 == 0:
            tap2_ref[frame // 2] = activated
            if frame // 2 + 1 < out_ref.shape[0]:
                tap0_ref[frame // 2 + 1] = activated
        else:
            tap1_ref[(frame + 1) // 2] = activated
    rows = out_ref.shape[0] * cols
    running = bias_ref[...]
    for time_tap, tap_ref in enumerate((tap0_ref, tap1_ref, tap2_ref)):
        block = tap_ref[...].reshape(rows, chans)
        running = running + jnp.dot(block, w_ref[time_tap], preferred_element_type=jnp.float32)
    out_ref[...] = running.astype(jnp.bfloat16).reshape(out_ref.shape)


def latent_call(frame_slots, received, w_time, totals, cell_count, norm_gain, norm_shift, time_bias, out_frames, cols):
    chans = w_time.shape[-1]
    vmem = pltpu.MemorySpace.VMEM if hasattr(pltpu, "MemorySpace") else pltpu.TPUMemorySpace.VMEM
    smem = pltpu.MemorySpace.SMEM if hasattr(pltpu, "MemorySpace") else pltpu.TPUMemorySpace.SMEM
    row = lambda v: v.reshape(1, chans).astype(jnp.float32)
    tap = pltpu.VMEM((out_frames, cols, chans), jnp.bfloat16)
    return pl.pallas_call(
        functools.partial(latent_kernel, cell_count=cell_count, groups=GROUPS),
        in_specs=[pl.BlockSpec(memory_space=smem)] + [pl.BlockSpec(memory_space=vmem)] * 6,
        out_specs=pl.BlockSpec(memory_space=vmem),
        out_shape=jax.ShapeDtypeStruct((out_frames, cols, chans), jnp.bfloat16),
        scratch_shapes=[tap, tap, tap],
    )(
        frame_slots, received, w_time,
        totals, row(norm_gain), row(norm_shift), row(time_bias),
    )

def spatial_conv(row_padded, w_spatial):
    out = lax.conv_general_dilated(
        row_padded,
        w_spatial,
        window_strides=(1, 1),
        padding=((0, 0), (1, 1)),
        dimension_numbers=("NHWC", "HWIO", "NHWC"),
        preferred_element_type=jnp.float32,
    )
    return out.astype(jnp.bfloat16)


def group_stats(conv_out, weight):
    cout_width = conv_out.shape[-1]
    per_group = cout_width // GROUPS
    values = conv_out.astype(jnp.float32).reshape(-1, cout_width)
    sums = jnp.sum(values, axis=0).reshape(GROUPS, per_group).sum(axis=1) * weight
    squares = jnp.sum(values * values, axis=0).reshape(GROUPS, per_group).sum(axis=1) * weight
    return sums, squares


def normalize(conv_out, sums, squares, cell_count, norm_gain, norm_shift):
    per_group = conv_out.shape[-1] // GROUPS
    group_mean = sums / cell_count
    group_var = squares / cell_count - group_mean * group_mean
    inv_scale = lax.rsqrt(group_var + 1e-06)
    mean_chan = jnp.repeat(group_mean, per_group)
    scale_chan = jnp.repeat(inv_scale, per_group)
    values = conv_out.astype(jnp.float32)
    return jax.nn.silu((values - mean_chan) * scale_chan * norm_gain + norm_shift).astype(
        jnp.bfloat16
    )


def time_conv(activated, w_time, time_bias, out_frames):
    first = activated[0:1]
    even = activated[0::2][:out_frames]
    odd = activated[1::2][: out_frames - 1]
    taps = [
        jnp.concatenate([first, even[: out_frames - 1]], axis=0),
        jnp.concatenate([first, odd], axis=0),
        even,
    ]
    stacked = jnp.concatenate(taps, axis=-1)
    weights = w_time.reshape(-1, w_time.shape[-1])
    product = jnp.einsum("trwc,cd->trwd", stacked, weights, preferred_element_type=jnp.float32)
    return (product + time_bias).astype(jnp.bfloat16)


def encode_stats(stats):
    high = stats.astype(jnp.bfloat16)
    low = (stats - high.astype(jnp.float32)).astype(jnp.bfloat16)
    return jnp.concatenate([high, low])


def decode_stats(coded, width):
    values = coded.astype(jnp.float32)
    return jnp.sum(values[:, :width], axis=0) + jnp.sum(values[:, width : 2 * width], axis=0)


def shards(clip_frames, frame_of_slot, w_spatial, norm_gain, norm_shift, w_time, time_bias):
    tm_count = lax.axis_size("tm")
    height_count = lax.axis_size("height")
    live_frames = tm_count // 2 + 1
    out_frames = (live_frames - 1) // 2 + 1
    frame_slots = slot_lookup(frame_of_slot, live_frames)
    count = lax.axis_size("height")
    forward = [(i, i + 1) for i in range(count - 1)]
    backward = [(target, source) for source, target in forward]
    low = lax.ppermute(clip_frames[0, -1:], "height", forward)
    high = lax.ppermute(clip_frames[0, :1], "height", backward)
    staged, _, _, coded = conv_call(frame_of_slot, low, high, clip_frames[0], w_spatial)
    cols = clip_frames.shape[2]
    tail = staged.shape[1] - 1
    per_group = w_spatial.shape[-1] // GROUPS
    column = coded[0]
    payload = staged.at[:, tail, :].set(jnp.broadcast_to(column, (staged.shape[0], column.shape[0])))
    payload, frame_slots = lax.optimization_barrier((payload, frame_slots))
    received = lax.all_to_all(payload[None], "tm", split_axis=1, concat_axis=0, tiled=True)
    partial = decode_stats(received[:, 0, tail, :], 2 * GROUPS)
    other = lax.ppermute(partial, "height", [(0, 1), (1, 0)])
    totals = partial + other
    cell_count = float(live_frames * clip_frames.shape[1] * height_count * cols * per_group)
    padded_totals = jnp.zeros((1, 128), jnp.float32).at[0, : totals.shape[0]].set(totals)
    latent = latent_call(
        frame_slots.astype(jnp.int32),
        received.reshape(received.shape[0], tail + 1, -1),
        w_time,
        padded_totals,
        cell_count,
        norm_gain,
        norm_shift,
        time_bias,
        out_frames,
        cols,
    )
    latent = latent.reshape(out_frames, 1, cols, latent.shape[-1])
    return latent.reshape(out_frames, 1, latent.shape[1], latent.shape[2], latent.shape[3])


def solution(mesh):
    return jax.shard_map(
        shards,
        mesh=mesh,
        in_specs=(P(("dp", "tm"), "height", None, None), P("dp"), P(), P(), P(), P(), P()),
        out_specs=P("dp", "height", "tm", None, None),
        check_vma=False,
    )
```

```python
import functools

import jax
import jax.numpy as jnp
import numpy as np
from jax import lax
from jax.experimental import pallas as pl
from jax.experimental.pallas import tpu as pltpu
from jax.sharding import PartitionSpec as P

GROUPS = 32


def with_halo(block, sides, width):
    for axis, dim in sides:
        count = lax.axis_size(axis)
        forward = [(i, i + 1) for i in range(count - 1)]
        backward = [(target, source) for source, target in forward]
        low = lax.ppermute(
            lax.slice_in_dim(block, block.shape[dim] - width, None, axis=dim), axis, forward
        )
        high = lax.ppermute(lax.slice_in_dim(block, 0, width, axis=dim), axis, backward)
        block = jnp.concatenate([low, block, high], axis=dim)
    return block


def slot_lookup(frame_of_slot, live_frames):
    wanted = jnp.arange(live_frames, dtype=jnp.int32)[:, None]
    places = jnp.arange(frame_of_slot.shape[0], dtype=jnp.int32)[None, :]
    matches = frame_of_slot[None, :] == wanted
    return jnp.sum(jnp.where(matches, places, 0), axis=1)


def conv_kernel(fos_ref, low_ref, high_ref, block_ref, w_ref, out_ref, sum_ref, sq_ref, code_ref, x_ref, sem, *, chunk, cols, groups):
    step = pl.program_id(0)
    rows = block_ref.shape[0]

    @pl.when(step == 0)
    def _():
        fetch = pltpu.make_async_copy(block_ref, x_ref.at[pl.ds(1, rows)], sem)
        fetch.start()
        x_ref[0:1] = low_ref[...]
        x_ref[rows + 1 : rows + 2] = high_ref[...]
        fetch.wait()

    base = step * chunk
    m = chunk * cols
    parts = []
    for col_tap in range(3):
        acc = None
        for row_tap in range(3):
            xs = x_ref[pl.ds(base + row_tap, chunk), :, :].reshape(m, x_ref.shape[-1])
            p = jnp.dot(xs, w_ref[row_tap, col_tap], preferred_element_type=jnp.float32)
            acc = p if acc is None else acc + p
        parts.append(acc)
    col = lax.broadcasted_iota(jnp.int32, (m, 1), 0) % cols
    left = jnp.where(col == 0, 0.0, pltpu.roll(parts[0], 1, 0))
    right = jnp.where(col == cols - 1, 0.0, pltpu.roll(parts[2], m - 1, 0))
    total = (left + parts[1]) + right
    rounded = total.astype(jnp.bfloat16)
    lanes = out_ref.shape[-1]
    for quarter in range(rounded.shape[-1] // lanes):
        piece = rounded[:, quarter * lanes : (quarter + 1) * lanes]
        out_ref[:, quarter * cols : (quarter + 1) * cols, :] = piece.reshape(chunk, cols, lanes)
    tail = out_ref.shape[1] - 1
    out_ref[:, tail : tail + 1, :] = jnp.zeros((chunk, 1, lanes), jnp.bfloat16)
    values = rounded.astype(jnp.float32)

    @pl.when(step == 0)
    def _():
        sum_ref[...] = jnp.zeros_like(sum_ref)
        sq_ref[...] = jnp.zeros_like(sq_ref)

    sum_ref[...] += jnp.sum(values, axis=0, keepdims=True)
    sq_ref[...] += jnp.sum(values * values, axis=0, keepdims=True)

    @pl.when(step == pl.num_programs(0) - 1)
    def _():
        chans = sum_ref.shape[-1]
        width = code_ref.shape[-1]
        per_group = chans // groups
        chan = lax.broadcasted_iota(jnp.int32, (chans, width), 0) // per_group
        lane = lax.broadcasted_iota(jnp.int32, (chans, width), 1)
        to_sums = jnp.where(chan == lane, 1.0, 0.0)
        to_squares = jnp.where(chan + groups == lane, 1.0, 0.0)
        exact = lax.Precision.HIGHEST
        grouped = jnp.dot(sum_ref[...], to_sums, precision=exact, preferred_element_type=jnp.float32)
        grouped = grouped + jnp.dot(sq_ref[...], to_squares, precision=exact, preferred_element_type=jnp.float32)
        own = fos_ref[lax.axis_index("tm")]
        grouped = grouped * jnp.where(own >= 0, 1.0, 0.0)
        high = grouped.astype(jnp.bfloat16).astype(jnp.float32)
        low = pltpu.roll(grouped - high, 2 * groups, 1)
        out_lane = lax.broadcasted_iota(jnp.int32, (1, width), 1)
        code_ref[...] = jnp.where(out_lane < 2 * groups, high, low).astype(jnp.bfloat16)

def conv_call(frame_of_slot, low, high, block, w, chunk=16, lanes=128):
    rows, cols, cin = block.shape
    cout = w.shape[-1]
    stacked = cols * (cout // lanes) + 1
    halo = pl.BlockSpec((1, cols, cin), lambda i: (0, 0, 0))
    return pl.pallas_call(
        functools.partial(conv_kernel, chunk=chunk, cols=cols, groups=GROUPS),
        grid=(rows // chunk,),
        in_specs=[
            pl.BlockSpec(memory_space=pltpu.SMEM),
            halo,
            halo,
            pl.BlockSpec(memory_space=pl.ANY),
            pl.BlockSpec((3, 3, cin, cout), lambda i: (0, 0, 0, 0)),
        ],
        out_specs=[
            pl.BlockSpec((chunk, stacked, lanes), lambda i: (i, 0, 0)),
            pl.BlockSpec((1, cout), lambda i: (0, 0)),
            pl.BlockSpec((1, cout), lambda i: (0, 0)),
            pl.BlockSpec((1, lanes), lambda i: (0, 0)),
        ],
        out_shape=[
            jax.ShapeDtypeStruct((rows, stacked, lanes), jnp.bfloat16),
            jax.ShapeDtypeStruct((1, cout), jnp.float32),
            jax.ShapeDtypeStruct((1, cout), jnp.float32),
            jax.ShapeDtypeStruct((1, lanes), jnp.bfloat16),
        ],
        scratch_shapes=[pltpu.VMEM((rows + 2, cols, cin), block.dtype), pltpu.SemaphoreType.DMA(())],
        compiler_params=pltpu.CompilerParams(dimension_semantics=("arbitrary",)),
    )(frame_of_slot, low, high, block, w)

def latent_kernel(slots_ref, x_ref, w_ref, totals_ref, gain_ref, shift_ref, bias_ref, out_ref, tap0_ref, tap1_ref, tap2_ref, *, cell_count, groups):
    live = 2 * out_ref.shape[0] - 1
    cols, chans = out_ref.shape[1], out_ref.shape[2]
    width = totals_ref.shape[-1]
    totals = totals_ref[...]
    lane = lax.broadcasted_iota(jnp.int32, (1, width), 1)
    group_mean = totals / cell_count
    group_var = pltpu.roll(totals, width - groups, 1) / cell_count - group_mean * group_mean
    inv_scale = lax.rsqrt(group_var + 1e-06)
    group_mean = jnp.where(lane < groups, group_mean, 0.0)
    inv_scale = jnp.where(lane < groups, inv_scale, 0.0)
    owner = lax.broadcasted_iota(jnp.int32, (width, chans), 1) // (chans // groups)
    expand = jnp.where(owner == lax.broadcasted_iota(jnp.int32, (width, chans), 0), 1.0, 0.0)
    exact = lax.Precision.HIGHEST
    mean_chan = jnp.dot(group_mean, expand, precision=exact, preferred_element_type=jnp.float32)
    scale_chan = jnp.dot(inv_scale, expand, precision=exact, preferred_element_type=jnp.float32)
    for frame in range(live):
        slot = slots_ref[frame]
        lanes = x_ref.shape[-1]
        pieces = [x_ref[slot, pl.ds(q * cols, cols), :] for q in range(chans // lanes)]
        values = jnp.concatenate(pieces, axis=-1).astype(jnp.float32)
        normed = (values - mean_chan) * scale_chan * gain_ref[...] + shift_ref[...]
        activated = jax.nn.silu(normed).astype(jnp.bfloat16)
        if frame == 0:
            tap0_ref[0] = activated
            tap1_ref[0] = activated
        if frame % 2 == 0:
            tap2_ref[frame // 2] = activated
            if frame // 2 + 1 < out_ref.shape[0]:
                tap0_ref[frame // 2 + 1] = activated
        else:
            tap1_ref[(frame + 1) // 2] = activated
    rows = out_ref.shape[0] * cols
    running = bias_ref[...]
    for time_tap, tap_ref in enumerate((tap0_ref, tap1_ref, tap2_ref)):
        block = tap_ref[...].reshape(rows, chans)
        running = running + jnp.dot(block, w_ref[time_tap], preferred_element_type=jnp.float32)
    out_ref[...] = running.astype(jnp.bfloat16).reshape(out_ref.shape)


def latent_call(frame_slots, received, w_time, totals, cell_count, norm_gain, norm_shift, time_bias, out_frames, cols):
    chans = w_time.shape[-1]
    vmem = pltpu.MemorySpace.VMEM if hasattr(pltpu, "MemorySpace") else pltpu.TPUMemorySpace.VMEM
    smem = pltpu.MemorySpace.SMEM if hasattr(pltpu, "MemorySpace") else pltpu.TPUMemorySpace.SMEM
    row = lambda v: v.reshape(1, chans).astype(jnp.float32)
    tap = pltpu.VMEM((out_frames, cols, chans), jnp.bfloat16)
    return pl.pallas_call(
        functools.partial(latent_kernel, cell_count=cell_count, groups=GROUPS),
        in_specs=[pl.BlockSpec(memory_space=smem)] + [pl.BlockSpec(memory_space=vmem)] * 6,
        out_specs=pl.BlockSpec(memory_space=vmem),
        out_shape=jax.ShapeDtypeStruct((out_frames, cols, chans), jnp.bfloat16),
        scratch_shapes=[tap, tap, tap],
    )(
        frame_slots, received, w_time,
        totals, row(norm_gain), row(norm_shift), row(time_bias),
    )

def spatial_conv(row_padded, w_spatial):
    out = lax.conv_general_dilated(
        row_padded,
        w_spatial,
        window_strides=(1, 1),
        padding=((0, 0), (1, 1)),
        dimension_numbers=("NHWC", "HWIO", "NHWC"),
        preferred_element_type=jnp.float32,
    )
    return out.astype(jnp.bfloat16)


def group_stats(conv_out, weight):
    cout_width = conv_out.shape[-1]
    per_group = cout_width // GROUPS
    values = conv_out.astype(jnp.float32).reshape(-1, cout_width)
    sums = jnp.sum(values, axis=0).reshape(GROUPS, per_group).sum(axis=1) * weight
    squares = jnp.sum(values * values, axis=0).reshape(GROUPS, per_group).sum(axis=1) * weight
    return sums, squares


def normalize(conv_out, sums, squares, cell_count, norm_gain, norm_shift):
    per_group = conv_out.shape[-1] // GROUPS
    group_mean = sums / cell_count
    group_var = squares / cell_count - group_mean * group_mean
    inv_scale = lax.rsqrt(group_var + 1e-06)
    mean_chan = jnp.repeat(group_mean, per_group)
    scale_chan = jnp.repeat(inv_scale, per_group)
    values = conv_out.astype(jnp.float32)
    return jax.nn.silu((values - mean_chan) * scale_chan * norm_gain + norm_shift).astype(
        jnp.bfloat16
    )


def time_conv(activated, w_time, time_bias, out_frames):
    first = activated[0:1]
    even = activated[0::2][:out_frames]
    odd = activated[1::2][: out_frames - 1]
    taps = [
        jnp.concatenate([first, even[: out_frames - 1]], axis=0),
        jnp.concatenate([first, odd], axis=0),
        even,
    ]
    stacked = jnp.concatenate(taps, axis=-1)
    weights = w_time.reshape(-1, w_time.shape[-1])
    product = jnp.einsum("trwc,cd->trwd", stacked, weights, preferred_element_type=jnp.float32)
    return (product + time_bias).astype(jnp.bfloat16)


def encode_stats(stats):
    high = stats.astype(jnp.bfloat16)
    low = (stats - high.astype(jnp.float32)).astype(jnp.bfloat16)
    return jnp.concatenate([high, low])


def decode_stats(coded, width):
    values = coded.astype(jnp.float32)
    return jnp.sum(values[:, :width], axis=0) + jnp.sum(values[:, width : 2 * width], axis=0)


def shards(clip_frames, frame_of_slot, w_spatial, norm_gain, norm_shift, w_time, time_bias):
    tm_count = lax.axis_size("tm")
    height_count = lax.axis_size("height")
    live_frames = tm_count // 2 + 1
    out_frames = (live_frames - 1) // 2 + 1
    frame_slots = slot_lookup(frame_of_slot, live_frames)
    count = lax.axis_size("height")
    forward = [(i, i + 1) for i in range(count - 1)]
    backward = [(target, source) for source, target in forward]
    low = lax.ppermute(clip_frames[0, -1:], "height", forward)
    high = lax.ppermute(clip_frames[0, :1], "height", backward)
    staged, _, _, coded = conv_call(frame_of_slot, low, high, clip_frames[0], w_spatial)
    cols = clip_frames.shape[2]
    tail = staged.shape[1] - 1
    per_group = w_spatial.shape[-1] // GROUPS
    column = coded[0]
    payload = staged.at[:, tail, :].set(jnp.broadcast_to(column, (staged.shape[0], column.shape[0])))
    payload, frame_slots = lax.optimization_barrier((payload, frame_slots))
    received = lax.all_to_all(payload[None], "tm", split_axis=1, concat_axis=0, tiled=True)
    partial = decode_stats(received[:, 0, tail, :], 2 * GROUPS)
    other = lax.ppermute(partial, "height", [(0, 1), (1, 0)])
    totals = partial + other
    cell_count = float(live_frames * clip_frames.shape[1] * height_count * cols * per_group)
    padded_totals = jnp.zeros((1, 128), jnp.float32).at[0, : totals.shape[0]].set(totals)
    latent = latent_call(
        frame_slots.astype(jnp.int32),
        received.reshape(received.shape[0], tail + 1, -1),
        w_time,
        padded_totals,
        cell_count,
        norm_gain,
        norm_shift,
        time_bias,
        out_frames,
        cols,
    )
    latent = latent.reshape(out_frames, 1, cols, latent.shape[-1])
    return latent.reshape(out_frames, 1, latent.shape[1], latent.shape[2], latent.shape[3])


def solution(mesh):
    return jax.shard_map(
        shards,
        mesh=mesh,
        in_specs=(P(("dp", "tm"), "height", None, None), P("dp"), P(), P(), P(), P(), P()),
        out_specs=P("dp", "height", "tm", None, None),
        check_vma=False,
    )
```

```python
import functools

import jax
import jax.numpy as jnp
import numpy as np
from jax import lax
from jax.experimental import pallas as pl
from jax.experimental.pallas import tpu as pltpu
from jax.sharding import PartitionSpec as P

GROUPS = 32


def with_halo(block, sides, width):
    for axis, dim in sides:
        count = lax.axis_size(axis)
        forward = [(i, i + 1) for i in range(count - 1)]
        backward = [(target, source) for source, target in forward]
        low = lax.ppermute(
            lax.slice_in_dim(block, block.shape[dim] - width, None, axis=dim), axis, forward
        )
        high = lax.ppermute(lax.slice_in_dim(block, 0, width, axis=dim), axis, backward)
        block = jnp.concatenate([low, block, high], axis=dim)
    return block


def slot_lookup(frame_of_slot, live_frames):
    wanted = jnp.arange(live_frames, dtype=jnp.int32)[:, None]
    places = jnp.arange(frame_of_slot.shape[0], dtype=jnp.int32)[None, :]
    matches = frame_of_slot[None, :] == wanted
    return jnp.sum(jnp.where(matches, places, 0), axis=1)


def conv_kernel(fos_ref, low_ref, high_ref, block_ref, w_ref, out_ref, sum_ref, sq_ref, code_ref, x_ref, sem, *, chunk, cols, groups):
    step = pl.program_id(0)
    rows = block_ref.shape[0]

    @pl.when(step == 0)
    def _():
        fetch = pltpu.make_async_copy(block_ref, x_ref.at[pl.ds(1, rows)], sem)
        fetch.start()
        x_ref[0:1] = low_ref[...]
        x_ref[rows + 1 : rows + 2] = high_ref[...]
        fetch.wait()

    base = step * chunk
    m = chunk * cols
    parts = []
    for col_tap in range(3):
        acc = None
        for row_tap in range(3):
            xs = x_ref[pl.ds(base + row_tap, chunk), :, :].reshape(m, x_ref.shape[-1])
            p = jnp.dot(xs, w_ref[row_tap, col_tap], preferred_element_type=jnp.float32)
            acc = p if acc is None else acc + p
        parts.append(acc)
    col = lax.broadcasted_iota(jnp.int32, (m, 1), 0) % cols
    left = jnp.where(col == 0, 0.0, pltpu.roll(parts[0], 1, 0))
    right = jnp.where(col == cols - 1, 0.0, pltpu.roll(parts[2], m - 1, 0))
    total = (left + parts[1]) + right
    rounded = total.astype(jnp.bfloat16)
    lanes = out_ref.shape[-1]
    for quarter in range(rounded.shape[-1] // lanes):
        piece = rounded[:, quarter * lanes : (quarter + 1) * lanes]
        out_ref[:, quarter * cols : (quarter + 1) * cols, :] = piece.reshape(chunk, cols, lanes)
    tail = out_ref.shape[1] - 1
    out_ref[:, tail : tail + 1, :] = jnp.zeros((chunk, 1, lanes), jnp.bfloat16)
    values = rounded.astype(jnp.float32)

    @pl.when(step == 0)
    def _():
        sum_ref[...] = jnp.zeros_like(sum_ref)
        sq_ref[...] = jnp.zeros_like(sq_ref)

    sum_ref[...] += jnp.sum(values, axis=0, keepdims=True)
    sq_ref[...] += jnp.sum(values * values, axis=0, keepdims=True)

    @pl.when(step == pl.num_programs(0) - 1)
    def _():
        chans = sum_ref.shape[-1]
        width = code_ref.shape[-1]
        per_group = chans // groups
        chan = lax.broadcasted_iota(jnp.int32, (chans, width), 0) // per_group
        lane = lax.broadcasted_iota(jnp.int32, (chans, width), 1)
        to_sums = jnp.where(chan == lane, 1.0, 0.0)
        to_squares = jnp.where(chan + groups == lane, 1.0, 0.0)
        exact = lax.Precision.HIGHEST
        grouped = jnp.dot(sum_ref[...], to_sums, precision=exact, preferred_element_type=jnp.float32)
        grouped = grouped + jnp.dot(sq_ref[...], to_squares, precision=exact, preferred_element_type=jnp.float32)
        own = fos_ref[lax.axis_index("tm")]
        grouped = grouped * jnp.where(own >= 0, 1.0, 0.0)
        high = grouped.astype(jnp.bfloat16).astype(jnp.float32)
        low = pltpu.roll(grouped - high, 2 * groups, 1)
        out_lane = lax.broadcasted_iota(jnp.int32, (1, width), 1)
        code_ref[...] = jnp.where(out_lane < 2 * groups, high, low).astype(jnp.bfloat16)

def conv_call(frame_of_slot, low, high, block, w, chunk=8, lanes=128):
    rows, cols, cin = block.shape
    cout = w.shape[-1]
    stacked = cols * (cout // lanes) + 1
    halo = pl.BlockSpec((1, cols, cin), lambda i: (0, 0, 0))
    return pl.pallas_call(
        functools.partial(conv_kernel, chunk=chunk, cols=cols, groups=GROUPS),
        grid=(rows // chunk,),
        in_specs=[
            pl.BlockSpec(memory_space=pltpu.SMEM),
            halo,
            halo,
            pl.BlockSpec(memory_space=pl.ANY),
            pl.BlockSpec((3, 3, cin, cout), lambda i: (0, 0, 0, 0)),
        ],
        out_specs=[
            pl.BlockSpec((chunk, stacked, lanes), lambda i: (i, 0, 0)),
            pl.BlockSpec((1, cout), lambda i: (0, 0)),
            pl.BlockSpec((1, cout), lambda i: (0, 0)),
            pl.BlockSpec((1, lanes), lambda i: (0, 0)),
        ],
        out_shape=[
            jax.ShapeDtypeStruct((rows, stacked, lanes), jnp.bfloat16),
            jax.ShapeDtypeStruct((1, cout), jnp.float32),
            jax.ShapeDtypeStruct((1, cout), jnp.float32),
            jax.ShapeDtypeStruct((1, lanes), jnp.bfloat16),
        ],
        scratch_shapes=[pltpu.VMEM((rows + 2, cols, cin), block.dtype), pltpu.SemaphoreType.DMA(())],
        compiler_params=pltpu.CompilerParams(dimension_semantics=("arbitrary",)),
    )(frame_of_slot, low, high, block, w)

def latent_kernel(slots_ref, src_ref, w_ref, totals_ref, gain_ref, shift_ref, bias_ref, out_ref, tap0_ref, tap1_ref, tap2_ref, x_ref, sems, *, cell_count, groups):
    live = 2 * out_ref.shape[0] - 1
    cols, chans = out_ref.shape[1], out_ref.shape[2]
    span = x_ref.shape[1]
    fetches = [
        pltpu.make_async_copy(src_ref.at[slots_ref[frame], pl.ds(0, span)], x_ref.at[frame], sems.at[frame])
        for frame in range(live)
    ]
    for fetch in fetches:
        fetch.start()
    width = totals_ref.shape[-1]
    totals = totals_ref[...]
    lane = lax.broadcasted_iota(jnp.int32, (1, width), 1)
    group_mean = totals / cell_count
    group_var = pltpu.roll(totals, width - groups, 1) / cell_count - group_mean * group_mean
    inv_scale = lax.rsqrt(group_var + 1e-06)
    group_mean = jnp.where(lane < groups, group_mean, 0.0)
    inv_scale = jnp.where(lane < groups, inv_scale, 0.0)
    owner = lax.broadcasted_iota(jnp.int32, (width, chans), 1) // (chans // groups)
    expand = jnp.where(owner == lax.broadcasted_iota(jnp.int32, (width, chans), 0), 1.0, 0.0)
    exact = lax.Precision.HIGHEST
    mean_chan = jnp.dot(group_mean, expand, precision=exact, preferred_element_type=jnp.float32)
    scale_chan = jnp.dot(inv_scale, expand, precision=exact, preferred_element_type=jnp.float32)
    for frame in range(live):
        fetches[frame].wait()
        lanes = x_ref.shape[-1]
        pieces = [x_ref[frame, pl.ds(q * cols, cols), :] for q in range(chans // lanes)]
        values = jnp.concatenate(pieces, axis=-1).astype(jnp.float32)
        normed = (values - mean_chan) * scale_chan * gain_ref[...] + shift_ref[...]
        activated = jax.nn.silu(normed).astype(jnp.bfloat16)
        if frame == 0:
            tap0_ref[0] = activated
            tap1_ref[0] = activated
        if frame % 2 == 0:
            tap2_ref[frame // 2] = activated
            if frame // 2 + 1 < out_ref.shape[0]:
                tap0_ref[frame // 2 + 1] = activated
        else:
            tap1_ref[(frame + 1) // 2] = activated
    rows = out_ref.shape[0] * cols
    running = bias_ref[...]
    for time_tap, tap_ref in enumerate((tap0_ref, tap1_ref, tap2_ref)):
        block = tap_ref[...].reshape(rows, chans)
        running = running + jnp.dot(block, w_ref[time_tap], preferred_element_type=jnp.float32)
    out_ref[...] = running.astype(jnp.bfloat16).reshape(out_ref.shape)


def latent_call(frame_slots, received, w_time, totals, cell_count, norm_gain, norm_shift, time_bias, out_frames, cols):
    chans = w_time.shape[-1]
    vmem = pltpu.MemorySpace.VMEM if hasattr(pltpu, "MemorySpace") else pltpu.TPUMemorySpace.VMEM
    smem = pltpu.MemorySpace.SMEM if hasattr(pltpu, "MemorySpace") else pltpu.TPUMemorySpace.SMEM
    row = lambda v: v.reshape(1, chans).astype(jnp.float32)
    tap = pltpu.VMEM((out_frames, cols, chans), jnp.bfloat16)
    return pl.pallas_call(
        functools.partial(latent_kernel, cell_count=cell_count, groups=GROUPS),
        in_specs=[pl.BlockSpec(memory_space=smem), pl.BlockSpec(memory_space=pl.ANY)]
        + [pl.BlockSpec(memory_space=vmem)] * 5,
        out_specs=pl.BlockSpec(memory_space=vmem),
        out_shape=jax.ShapeDtypeStruct((out_frames, cols, chans), jnp.bfloat16),
        scratch_shapes=[
            tap,
            tap,
            tap,
            pltpu.VMEM((2 * out_frames - 1, cols * (chans // received.shape[-1]), received.shape[-1]), received.dtype),
            pltpu.SemaphoreType.DMA((2 * out_frames - 1,)),
        ],
    )(
        frame_slots, received, w_time,
        totals, row(norm_gain), row(norm_shift), row(time_bias),
    )

def spatial_conv(row_padded, w_spatial):
    out = lax.conv_general_dilated(
        row_padded,
        w_spatial,
        window_strides=(1, 1),
        padding=((0, 0), (1, 1)),
        dimension_numbers=("NHWC", "HWIO", "NHWC"),
        preferred_element_type=jnp.float32,
    )
    return out.astype(jnp.bfloat16)


def group_stats(conv_out, weight):
    cout_width = conv_out.shape[-1]
    per_group = cout_width // GROUPS
    values = conv_out.astype(jnp.float32).reshape(-1, cout_width)
    sums = jnp.sum(values, axis=0).reshape(GROUPS, per_group).sum(axis=1) * weight
    squares = jnp.sum(values * values, axis=0).reshape(GROUPS, per_group).sum(axis=1) * weight
    return sums, squares


def normalize(conv_out, sums, squares, cell_count, norm_gain, norm_shift):
    per_group = conv_out.shape[-1] // GROUPS
    group_mean = sums / cell_count
    group_var = squares / cell_count - group_mean * group_mean
    inv_scale = lax.rsqrt(group_var + 1e-06)
    mean_chan = jnp.repeat(group_mean, per_group)
    scale_chan = jnp.repeat(inv_scale, per_group)
    values = conv_out.astype(jnp.float32)
    return jax.nn.silu((values - mean_chan) * scale_chan * norm_gain + norm_shift).astype(
        jnp.bfloat16
    )


def time_conv(activated, w_time, time_bias, out_frames):
    first = activated[0:1]
    even = activated[0::2][:out_frames]
    odd = activated[1::2][: out_frames - 1]
    taps = [
        jnp.concatenate([first, even[: out_frames - 1]], axis=0),
        jnp.concatenate([first, odd], axis=0),
        even,
    ]
    stacked = jnp.concatenate(taps, axis=-1)
    weights = w_time.reshape(-1, w_time.shape[-1])
    product = jnp.einsum("trwc,cd->trwd", stacked, weights, preferred_element_type=jnp.float32)
    return (product + time_bias).astype(jnp.bfloat16)


def encode_stats(stats):
    high = stats.astype(jnp.bfloat16)
    low = (stats - high.astype(jnp.float32)).astype(jnp.bfloat16)
    return jnp.concatenate([high, low])


def decode_stats(coded, width):
    values = coded.astype(jnp.float32)
    return jnp.sum(values[:, :width], axis=0) + jnp.sum(values[:, width : 2 * width], axis=0)


def shards(clip_frames, frame_of_slot, w_spatial, norm_gain, norm_shift, w_time, time_bias):
    tm_count = lax.axis_size("tm")
    height_count = lax.axis_size("height")
    live_frames = tm_count // 2 + 1
    out_frames = (live_frames - 1) // 2 + 1
    frame_slots = slot_lookup(frame_of_slot, live_frames)
    count = lax.axis_size("height")
    forward = [(i, i + 1) for i in range(count - 1)]
    backward = [(target, source) for source, target in forward]
    low = lax.ppermute(clip_frames[0, -1:], "height", forward)
    high = lax.ppermute(clip_frames[0, :1], "height", backward)
    staged, _, _, coded = conv_call(frame_of_slot, low, high, clip_frames[0], w_spatial)
    cols = clip_frames.shape[2]
    tail = staged.shape[1] - 1
    per_group = w_spatial.shape[-1] // GROUPS
    column = coded[0]
    payload = staged.at[:, tail, :].set(jnp.broadcast_to(column, (staged.shape[0], column.shape[0])))
    payload, frame_slots = lax.optimization_barrier((payload, frame_slots))
    received = lax.all_to_all(payload[None], "tm", split_axis=1, concat_axis=0, tiled=True)
    partial = decode_stats(received[:, 0, tail, :], 2 * GROUPS)
    other = lax.ppermute(partial, "height", [(0, 1), (1, 0)])
    totals = partial + other
    cell_count = float(live_frames * clip_frames.shape[1] * height_count * cols * per_group)
    padded_totals = jnp.zeros((1, 128), jnp.float32).at[0, : totals.shape[0]].set(totals)
    latent = latent_call(
        frame_slots.astype(jnp.int32),
        received.reshape(received.shape[0], tail + 1, -1),
        w_time,
        padded_totals,
        cell_count,
        norm_gain,
        norm_shift,
        time_bias,
        out_frames,
        cols,
    )
    latent = latent.reshape(out_frames, 1, cols, latent.shape[-1])
    return latent.reshape(out_frames, 1, latent.shape[1], latent.shape[2], latent.shape[3])


def solution(mesh):
    return jax.shard_map(
        shards,
        mesh=mesh,
        in_specs=(P(("dp", "tm"), "height", None, None), P("dp"), P(), P(), P(), P(), P()),
        out_specs=P("dp", "height", "tm", None, None),
        check_vma=False,
    )
```

```python
import functools

import jax
import jax.numpy as jnp
import numpy as np
from jax import lax
from jax.experimental import pallas as pl
from jax.experimental.pallas import tpu as pltpu
from jax.sharding import PartitionSpec as P

GROUPS = 32


def with_halo(block, sides, width):
    for axis, dim in sides:
        count = lax.axis_size(axis)
        forward = [(i, i + 1) for i in range(count - 1)]
        backward = [(target, source) for source, target in forward]
        low = lax.ppermute(
            lax.slice_in_dim(block, block.shape[dim] - width, None, axis=dim), axis, forward
        )
        high = lax.ppermute(lax.slice_in_dim(block, 0, width, axis=dim), axis, backward)
        block = jnp.concatenate([low, block, high], axis=dim)
    return block


def slot_lookup(frame_of_slot, live_frames):
    wanted = jnp.arange(live_frames, dtype=jnp.int32)[:, None]
    places = jnp.arange(frame_of_slot.shape[0], dtype=jnp.int32)[None, :]
    matches = frame_of_slot[None, :] == wanted
    return jnp.sum(jnp.where(matches, places, 0), axis=1)


def conv_kernel(fos_ref, low_ref, high_ref, block_ref, w_ref, out_ref, sum_ref, sq_ref, code_ref, x_ref, sem, *, chunk, cols, groups):
    step = pl.program_id(0)
    rows = block_ref.shape[0]

    head = chunk + 1
    first = pltpu.make_async_copy(block_ref.at[pl.ds(0, head)], x_ref.at[pl.ds(1, head)], sem.at[0])
    rest = pltpu.make_async_copy(
        block_ref.at[pl.ds(head, rows - head)], x_ref.at[pl.ds(head + 1, rows - head)], sem.at[1]
    )

    @pl.when(step == 0)
    def _():
        first.start()
        rest.start()
        x_ref[0:1] = low_ref[...]
        x_ref[rows + 1 : rows + 2] = high_ref[...]
        first.wait()

    @pl.when(step == 1)
    def _():
        rest.wait()

    base = step * chunk
    m = chunk * cols
    parts = []
    for col_tap in range(3):
        acc = None
        for row_tap in range(3):
            xs = x_ref[pl.ds(base + row_tap, chunk), :, :].reshape(m, x_ref.shape[-1])
            p = jnp.dot(xs, w_ref[row_tap, col_tap], preferred_element_type=jnp.float32)
            acc = p if acc is None else acc + p
        parts.append(acc)
    col = lax.broadcasted_iota(jnp.int32, (m, 1), 0) % cols
    left = jnp.where(col == 0, 0.0, pltpu.roll(parts[0], 1, 0))
    right = jnp.where(col == cols - 1, 0.0, pltpu.roll(parts[2], m - 1, 0))
    total = (left + parts[1]) + right
    rounded = total.astype(jnp.bfloat16)
    lanes = out_ref.shape[-1]
    for quarter in range(rounded.shape[-1] // lanes):
        piece = rounded[:, quarter * lanes : (quarter + 1) * lanes]
        out_ref[:, quarter * cols : (quarter + 1) * cols, :] = piece.reshape(chunk, cols, lanes)
    tail = out_ref.shape[1] - 1
    out_ref[:, tail : tail + 1, :] = jnp.zeros((chunk, 1, lanes), jnp.bfloat16)
    values = rounded.astype(jnp.float32)

    @pl.when(step == 0)
    def _():
        sum_ref[...] = jnp.zeros_like(sum_ref)
        sq_ref[...] = jnp.zeros_like(sq_ref)

    sum_ref[...] += jnp.sum(values, axis=0, keepdims=True)
    sq_ref[...] += jnp.sum(values * values, axis=0, keepdims=True)

    @pl.when(step == pl.num_programs(0) - 1)
    def _():
        chans = sum_ref.shape[-1]
        width = code_ref.shape[-1]
        per_group = chans // groups
        chan = lax.broadcasted_iota(jnp.int32, (chans, width), 0) // per_group
        lane = lax.broadcasted_iota(jnp.int32, (chans, width), 1)
        to_sums = jnp.where(chan == lane, 1.0, 0.0)
        to_squares = jnp.where(chan + groups == lane, 1.0, 0.0)
        exact = lax.Precision.HIGHEST
        grouped = jnp.dot(sum_ref[...], to_sums, precision=exact, preferred_element_type=jnp.float32)
        grouped = grouped + jnp.dot(sq_ref[...], to_squares, precision=exact, preferred_element_type=jnp.float32)
        own = fos_ref[lax.axis_index("tm")]
        grouped = grouped * jnp.where(own >= 0, 1.0, 0.0)
        high = grouped.astype(jnp.bfloat16).astype(jnp.float32)
        low = pltpu.roll(grouped - high, 2 * groups, 1)
        out_lane = lax.broadcasted_iota(jnp.int32, (1, width), 1)
        code_ref[...] = jnp.where(out_lane < 2 * groups, high, low).astype(jnp.bfloat16)

def conv_call(frame_of_slot, low, high, block, w, chunk=8, lanes=128):
    rows, cols, cin = block.shape
    cout = w.shape[-1]
    stacked = cols * (cout // lanes) + 1
    halo = pl.BlockSpec((1, cols, cin), lambda i: (0, 0, 0))
    return pl.pallas_call(
        functools.partial(conv_kernel, chunk=chunk, cols=cols, groups=GROUPS),
        grid=(rows // chunk,),
        in_specs=[
            pl.BlockSpec(memory_space=pltpu.SMEM),
            halo,
            halo,
            pl.BlockSpec(memory_space=pl.ANY),
            pl.BlockSpec((3, 3, cin, cout), lambda i: (0, 0, 0, 0)),
        ],
        out_specs=[
            pl.BlockSpec((chunk, stacked, lanes), lambda i: (i, 0, 0)),
            pl.BlockSpec((1, cout), lambda i: (0, 0)),
            pl.BlockSpec((1, cout), lambda i: (0, 0)),
            pl.BlockSpec((1, lanes), lambda i: (0, 0)),
        ],
        out_shape=[
            jax.ShapeDtypeStruct((rows, stacked, lanes), jnp.bfloat16),
            jax.ShapeDtypeStruct((1, cout), jnp.float32),
            jax.ShapeDtypeStruct((1, cout), jnp.float32),
            jax.ShapeDtypeStruct((1, lanes), jnp.bfloat16),
        ],
        scratch_shapes=[pltpu.VMEM((rows + 2, cols, cin), block.dtype), pltpu.SemaphoreType.DMA((2,))],
        compiler_params=pltpu.CompilerParams(dimension_semantics=("arbitrary",)),
    )(frame_of_slot, low, high, block, w)

def latent_kernel(slots_ref, x_ref, w_ref, totals_ref, gain_ref, shift_ref, bias_ref, out_ref, tap0_ref, tap1_ref, tap2_ref, *, cell_count, groups):
    live = 2 * out_ref.shape[0] - 1
    cols, chans = out_ref.shape[1], out_ref.shape[2]
    width = totals_ref.shape[-1]
    totals = totals_ref[...]
    lane = lax.broadcasted_iota(jnp.int32, (1, width), 1)
    group_mean = totals / cell_count
    group_var = pltpu.roll(totals, width - groups, 1) / cell_count - group_mean * group_mean
    inv_scale = lax.rsqrt(group_var + 1e-06)
    group_mean = jnp.where(lane < groups, group_mean, 0.0)
    inv_scale = jnp.where(lane < groups, inv_scale, 0.0)
    owner = lax.broadcasted_iota(jnp.int32, (width, chans), 1) // (chans // groups)
    expand = jnp.where(owner == lax.broadcasted_iota(jnp.int32, (width, chans), 0), 1.0, 0.0)
    exact = lax.Precision.HIGHEST
    mean_chan = jnp.dot(group_mean, expand, precision=exact, preferred_element_type=jnp.float32)
    scale_chan = jnp.dot(inv_scale, expand, precision=exact, preferred_element_type=jnp.float32)
    for frame in range(live):
        slot = slots_ref[frame]
        lanes = x_ref.shape[-1]
        pieces = [x_ref[slot, pl.ds(q * cols, cols), :] for q in range(chans // lanes)]
        values = jnp.concatenate(pieces, axis=-1).astype(jnp.float32)
        normed = (values - mean_chan) * scale_chan * gain_ref[...] + shift_ref[...]
        activated = jax.nn.silu(normed).astype(jnp.bfloat16)
        if frame == 0:
            tap0_ref[0] = activated
            tap1_ref[0] = activated
        if frame % 2 == 0:
            tap2_ref[frame // 2] = activated
            if frame // 2 + 1 < out_ref.shape[0]:
                tap0_ref[frame // 2 + 1] = activated
        else:
            tap1_ref[(frame + 1) // 2] = activated
    rows = out_ref.shape[0] * cols
    running = bias_ref[...]
    for time_tap, tap_ref in enumerate((tap0_ref, tap1_ref, tap2_ref)):
        block = tap_ref[...].reshape(rows, chans)
        running = running + jnp.dot(block, w_ref[time_tap], preferred_element_type=jnp.float32)
    out_ref[...] = running.astype(jnp.bfloat16).reshape(out_ref.shape)


def latent_call(frame_slots, received, w_time, totals, cell_count, norm_gain, norm_shift, time_bias, out_frames, cols):
    chans = w_time.shape[-1]
    vmem = pltpu.MemorySpace.VMEM if hasattr(pltpu, "MemorySpace") else pltpu.TPUMemorySpace.VMEM
    smem = pltpu.MemorySpace.SMEM if hasattr(pltpu, "MemorySpace") else pltpu.TPUMemorySpace.SMEM
    row = lambda v: v.reshape(1, chans).astype(jnp.float32)
    tap = pltpu.VMEM((out_frames, cols, chans), jnp.bfloat16)
    return pl.pallas_call(
        functools.partial(latent_kernel, cell_count=cell_count, groups=GROUPS),
        in_specs=[pl.BlockSpec(memory_space=smem)] + [pl.BlockSpec(memory_space=vmem)] * 6,
        out_specs=pl.BlockSpec(memory_space=vmem),
        out_shape=jax.ShapeDtypeStruct((out_frames, cols, chans), jnp.bfloat16),
        scratch_shapes=[tap, tap, tap],
    )(
        frame_slots, received, w_time,
        totals, row(norm_gain), row(norm_shift), row(time_bias),
    )

def spatial_conv(row_padded, w_spatial):
    out = lax.conv_general_dilated(
        row_padded,
        w_spatial,
        window_strides=(1, 1),
        padding=((0, 0), (1, 1)),
        dimension_numbers=("NHWC", "HWIO", "NHWC"),
        preferred_element_type=jnp.float32,
    )
    return out.astype(jnp.bfloat16)


def group_stats(conv_out, weight):
    cout_width = conv_out.shape[-1]
    per_group = cout_width // GROUPS
    values = conv_out.astype(jnp.float32).reshape(-1, cout_width)
    sums = jnp.sum(values, axis=0).reshape(GROUPS, per_group).sum(axis=1) * weight
    squares = jnp.sum(values * values, axis=0).reshape(GROUPS, per_group).sum(axis=1) * weight
    return sums, squares


def normalize(conv_out, sums, squares, cell_count, norm_gain, norm_shift):
    per_group = conv_out.shape[-1] // GROUPS
    group_mean = sums / cell_count
    group_var = squares / cell_count - group_mean * group_mean
    inv_scale = lax.rsqrt(group_var + 1e-06)
    mean_chan = jnp.repeat(group_mean, per_group)
    scale_chan = jnp.repeat(inv_scale, per_group)
    values = conv_out.astype(jnp.float32)
    return jax.nn.silu((values - mean_chan) * scale_chan * norm_gain + norm_shift).astype(
        jnp.bfloat16
    )


def time_conv(activated, w_time, time_bias, out_frames):
    first = activated[0:1]
    even = activated[0::2][:out_frames]
    odd = activated[1::2][: out_frames - 1]
    taps = [
        jnp.concatenate([first, even[: out_frames - 1]], axis=0),
        jnp.concatenate([first, odd], axis=0),
        even,
    ]
    stacked = jnp.concatenate(taps, axis=-1)
    weights = w_time.reshape(-1, w_time.shape[-1])
    product = jnp.einsum("trwc,cd->trwd", stacked, weights, preferred_element_type=jnp.float32)
    return (product + time_bias).astype(jnp.bfloat16)


def encode_stats(stats):
    high = stats.astype(jnp.bfloat16)
    low = (stats - high.astype(jnp.float32)).astype(jnp.bfloat16)
    return jnp.concatenate([high, low])


def decode_stats(coded, width):
    values = coded.astype(jnp.float32)
    return jnp.sum(values[:, :width], axis=0) + jnp.sum(values[:, width : 2 * width], axis=0)


def shards(clip_frames, frame_of_slot, w_spatial, norm_gain, norm_shift, w_time, time_bias):
    tm_count = lax.axis_size("tm")
    height_count = lax.axis_size("height")
    live_frames = tm_count // 2 + 1
    out_frames = (live_frames - 1) // 2 + 1
    frame_slots = slot_lookup(frame_of_slot, live_frames)
    count = lax.axis_size("height")
    forward = [(i, i + 1) for i in range(count - 1)]
    backward = [(target, source) for source, target in forward]
    low = lax.ppermute(clip_frames[0, -1:], "height", forward)
    high = lax.ppermute(clip_frames[0, :1], "height", backward)
    staged, _, _, coded = conv_call(frame_of_slot, low, high, clip_frames[0], w_spatial)
    cols = clip_frames.shape[2]
    tail = staged.shape[1] - 1
    per_group = w_spatial.shape[-1] // GROUPS
    column = coded[0]
    payload = staged.at[:, tail, :].set(jnp.broadcast_to(column, (staged.shape[0], column.shape[0])))
    payload, frame_slots = lax.optimization_barrier((payload, frame_slots))
    received = lax.all_to_all(payload[None], "tm", split_axis=1, concat_axis=0, tiled=True)
    partial = decode_stats(received[:, 0, tail, :], 2 * GROUPS)
    other = lax.ppermute(partial, "height", [(0, 1), (1, 0)])
    totals = partial + other
    cell_count = float(live_frames * clip_frames.shape[1] * height_count * cols * per_group)
    padded_totals = jnp.zeros((1, 128), jnp.float32).at[0, : totals.shape[0]].set(totals)
    latent = latent_call(
        frame_slots.astype(jnp.int32),
        received.reshape(received.shape[0], tail + 1, -1),
        w_time,
        padded_totals,
        cell_count,
        norm_gain,
        norm_shift,
        time_bias,
        out_frames,
        cols,
    )
    latent = latent.reshape(out_frames, 1, cols, latent.shape[-1])
    return latent.reshape(out_frames, 1, latent.shape[1], latent.shape[2], latent.shape[3])


def solution(mesh):
    return jax.shard_map(
        shards,
        mesh=mesh,
        in_specs=(P(("dp", "tm"), "height", None, None), P("dp"), P(), P(), P(), P(), P()),
        out_specs=P("dp", "height", "tm", None, None),
        check_vma=False,
    )
```
